32 devices in a mesh: groups: 2 (over y), seq: 4 (over z), tensor: 4 (over x, core).
Axes of the slice: x: 2, y: 2, z: 4, core: 2. Of those that a mesh axis runs over, the one named last changes fastest.
Arguments:
- tree_query: bfloat16 [32, 64, 16384], P('groups', 'seq', 'tensor'), parts along dimension 0, may hold values from -20 to 20
- tree_key: bfloat16 [32, 64, 1024], P('groups', 'seq', 'tensor'), parts along dimension 0, may hold values from -4 to 4
- tree_value: bfloat16 [32, 64, 1024], P('groups', 'seq', 'tensor'), parts along dimension 0, may hold values from -6 to 6
- draft_logit: bfloat16 [32, 64], P('groups', 'seq'), parts along dimension 0, may hold values from -4 to 4
- cache_key: bfloat16 [32, 2048, 1024], P(('groups', 'seq'), None, 'tensor'), parts along dimension 0, may hold values from -6 to 6
- cache_value: bfloat16 [32, 2048, 1024], P(('groups', 'seq'), None, 'tensor'), parts along dimension 0, may hold values from -6 to 6
- score_weight: float32 [16384], P('tensor'), may hold values from -1.5 to 1.5
- serve_order: int32 [32], P('groups'), parts along dimension 0, may hold values from 0 to 15, each once
- lengths: int32 [32], P('groups'), parts along dimension 0, may hold values from 1 to 2048, 16384 in all
- parents: int32 [32, 64], P('groups'), parts along dimension 0, may hold values from -1 to 62, as said below
- ancestors: int32 [32, 64, 2], P('groups'), parts along dimension 0, may hold values from -2147483648 to 2147483647, as said below
Outputs:
- attn_out: bfloat16 [32, 64, 16384], P(('groups', 'seq'), None, 'tensor'), parts along dimension 0
- kl: float32 [32], P(('groups', 'seq')), parts along dimension 0
The draws below stay inside these ranges and needn't reach their ends.
There are 2 independent parts, one for each index of `groups`. The reference program is written for one: setup_inputs(seed, part) draws one part's arguments, and reference() takes and returns one part's arrays. A program takes and returns all parts, laid end to end along the dimension named above; an argument that names none is the same for every part. Nothing has to cross between parts.
Inputs may be any that keep to these rules, and one draw needn't show every extreme that they name: `parents`: node 0 is the root with parent -1; every other node n has a parent below n. `ancestors`: bit (m mod 32) of word m // 32 of node n's entry is 1 exactly when m is n or an ancestor of n under parents of the same request; words are read as signed 32-bit integers.
All inputs are finite; a program needn't handle non-finite values.
Results may differ from the reference program's by a relative error of at most 0.0044.
Values may be sent and summed in bfloat16 or wider, within the bound.
A program may use at most 128 MiB of HBM per device.

```python
import math
import jax
import jax.numpy as jnp
import numpy as np
from jax import lax

HEADS = 128
KVH = 8
HD = 128
NODES = 64
CACHE = 2048
R = 16


def tree_keys_base(key):
    drawn = jax.random.normal(jax.random.fold_in(key, 7), (R, NODES, KVH * HD), jnp.float32)
    return jnp.clip(drawn, -4.0, 4.0)


def tree_shape(key):
    node_ids = jnp.arange(NODES, dtype=jnp.int32)
    request_ids = jnp.arange(R, dtype=jnp.int32)[:, None]
    drawn = jax.random.randint(jax.random.fold_in(key, 21), (R, NODES), 0, jnp.maximum(node_ids, 1))
    chain = jnp.broadcast_to(node_ids - 1, (R, NODES))
    drawn = jnp.where(request_ids == 0, chain, jnp.where(request_ids == R - 1, 0, drawn))
    parent_ids = jnp.where(node_ids == 0, -1, drawn).astype(jnp.int32)
    mask_words = jnp.zeros((R, NODES, 2), jnp.int32)
    for node_id in range(NODES):
        self_bit = jnp.zeros((R, 2), jnp.int32).at[:, node_id // 32].set(jnp.left_shift(jnp.int32(1), jnp.int32(node_id % 32)))
        if node_id > 0:
            where_from = jnp.broadcast_to(parent_ids[:, node_id][:, None, None], (R, 1, 2))
            inherited = jnp.take_along_axis(mask_words, where_from, axis=1)[:, 0]
            self_bit = self_bit | inherited
        mask_words = mask_words.at[:, node_id].set(self_bit)
    return (parent_ids, mask_words)


def draw_tree_key(key, part):
    base = tree_keys_base(key)
    return jnp.clip(base, -4.0, 4.0).astype(jnp.bfloat16)


def draw_tree_query(key, part):
    base = jax.random.normal(jax.random.fold_in(key, 8), (R, NODES, HEADS * HD), jnp.float32)
    return jnp.clip(base, -20.0, 20.0).astype(jnp.bfloat16)


def draw_parents(key, part):
    return tree_shape(key)[0]


def draw_ancestors(key, part):
    return tree_shape(key)[1]


def block_levels(key, shape, split, low, top_value):
    def one(dim, blocks):
        draws = jax.random.uniform(jax.random.fold_in(jax.random.fold_in(key, 6), dim), (blocks,), jnp.float32, low / len(split), top_value / len(split))
        return jnp.repeat(jnp.exp(draws), shape[dim] // blocks).reshape((-1,) + (1,) * (len(shape) - dim - 1))

    factor_of = one(*split[0])
    for cut in split[1:]:
        factor_of = factor_of * one(*cut)
    return factor_of


def profile(count, total, limit, slope):
    portions = [(1 << 20) // math.isqrt(grade ** slope) + 1 for grade in range(2, count + 1)]
    spare, given = total - limit - (count - 1), [1] * (count - 1)
    while spare > 0:
        free = [i for i in range(count - 1) if given[i] < limit]
        pool, left = sum([portions[i] for i in free]), spare
        for i in free:
            addition = min(limit - given[i], max(1, left * portions[i] // pool), spare)
            given[i] = given[i] + addition
            spare = spare - addition
    return np.array([limit] + given)


def uneven(key, amount, total, limit, slope):
    if amount == 2:
        one = jax.random.randint(key, (), max(1, total - limit), min(limit, total - 1) + 1)
        return jnp.stack([one, total - one])
    tallies = jnp.asarray(profile(amount, total, limit, slope), jnp.int32)
    couples = (amount - 1) // 2
    donor, taker = tallies[1:1 + 2 * couples:2], tallies[2:2 + 2 * couples:2]
    slack = jnp.minimum(donor - 1, limit - taker)
    passed = jax.random.randint(jax.random.fold_in(key, 1), (couples,), 0, 1 << 20) % (slack + 1)
    tallies = tallies.at[1:1 + 2 * couples:2].set(donor - passed).at[2:2 + 2 * couples:2].set(taker + passed)
    return tallies[jax.random.permutation(jax.random.fold_in(key, 2), amount)]


def bell_draw(key, dims, spread, most, split=(), kind=jnp.bfloat16):
    entries = spread * jax.random.normal(key, dims, jnp.float32)
    if split:
        entries = entries * block_levels(key, dims, split, -0.22, 0.18)
    return jnp.clip(entries, -most, most).astype(kind)


def setup_inputs(seed: int = 0, part: int = 0) -> dict:
    key_list = jax.random.split(jax.random.key(seed), 12)
    own_keys = jax.random.split(jax.random.fold_in(key_list[11], part), 12)
    return {
        "tree_query": draw_tree_query(jax.random.fold_in(jax.random.fold_in(key_list[11], part), 71), part),
        "tree_key": draw_tree_key(jax.random.fold_in(jax.random.fold_in(key_list[11], part), 71), part),
        "tree_value": bell_draw(own_keys[2], (R, NODES, KVH * HD), 1.0, 6.0, ((1, 4), (2, 4))),
        "draft_logit": jnp.clip(jax.random.uniform(own_keys[3], (R, NODES), jnp.float32, -4.0, 4.0) * block_levels(own_keys[3], (R, NODES), ((1, 4),), -0.4, 0.0), -4.0, 4.0).astype(jnp.bfloat16),
        "cache_key": bell_draw(own_keys[4], (R, CACHE, KVH * HD), 1.0, 6.0, ((0, 4), (2, 4))),
        "cache_value": bell_draw(own_keys[5], (R, CACHE, KVH * HD), 1.0, 6.0, ((0, 4), (2, 4))),
        "score_weight": bell_draw(key_list[6], (HEADS * HD,), 0.25, 1.5, ((0, 4),), jnp.float32),
        "serve_order": jax.random.permutation(own_keys[7], R).astype(jnp.int32),
        "lengths": uneven(own_keys[8], R, R * CACHE // 2, CACHE, 2).astype(jnp.int32),
        "parents": draw_parents(jax.random.fold_in(jax.random.fold_in(key_list[11], part), 71), part),
        "ancestors": draw_ancestors(jax.random.fold_in(jax.random.fold_in(key_list[11], part), 71), part),
    }


def ancestor_bits(mask_words):
    node_ids = jnp.arange(NODES, dtype=jnp.int32)
    chosen = jnp.where(node_ids // 32 == 0, mask_words[..., 0:1], mask_words[..., 1:2])
    return (jnp.right_shift(chosen, node_ids % 32) & 1) == 1


def sibling_kl(head_score, drafted, parent_ids):
    groups = parent_ids + 1
    onehot = (groups[:, :, None] == jnp.arange(NODES, dtype=jnp.int32)).astype(jnp.float32)
    target = 4.0 * jnp.tanh(head_score / 4.0)
    hp = lax.Precision.HIGHEST
    target_sums = jnp.einsum('rnc,rn->rc', onehot, jnp.exp(target), precision=hp)
    draft_sums = jnp.einsum('rnc,rn->rc', onehot, jnp.exp(drafted), precision=hp)
    target_log = target - jnp.log(jnp.einsum('rnc,rc->rn', onehot, target_sums, precision=hp))
    draft_log = drafted - jnp.log(jnp.einsum('rnc,rc->rn', onehot, draft_sums, precision=hp))
    return jnp.sum(jnp.exp(target_log) * (target_log - draft_log), axis=1)


def reference(tree_query, tree_key, tree_value, draft_logit, cache_key, cache_value, score_weight, serve_order, lengths, parents, ancestors):
    group_size = HEADS // KVH
    softmax_scale = HD ** -0.5
    hp = lax.Precision.HIGHEST

    def one_slot(slot_id):
        request = serve_order[slot_id]
        queries = tree_query[request].astype(jnp.float32).reshape(NODES, KVH, group_size, HD)
        all_keys = jnp.concatenate([cache_key[slot_id], tree_key[request]], axis=0).astype(jnp.float32).reshape(CACHE + NODES, KVH, HD)
        all_values = jnp.concatenate([cache_value[slot_id], tree_value[request]], axis=0).astype(jnp.float32).reshape(CACHE + NODES, KVH, HD)
        cached = jnp.broadcast_to((jnp.arange(CACHE, dtype=jnp.int32) < lengths[request])[None, :], (NODES, CACHE))
        visible = jnp.concatenate([cached, ancestor_bits(ancestors[request])], axis=1)
        allowed = visible[None, :, None, :]
        scores = jnp.einsum('nkgd,ckd->kngc', queries, all_keys, precision=hp) * softmax_scale
        row_top = jnp.max(jnp.where(allowed, scores, -jnp.inf), axis=-1, keepdims=True)
        weights = jnp.where(allowed, jnp.exp(scores - row_top), 0.0)
        totals = jnp.sum(weights, axis=-1)
        rounded = lax.optimization_barrier(weights.astype(jnp.bfloat16)).astype(jnp.float32)
        attended = jnp.einsum('kngc,ckd->kngd', rounded, all_values, precision=hp) / totals[..., None]
        attended = jnp.transpose(attended, (1, 0, 2, 3)).reshape(NODES, HEADS * HD)
        head_score = jnp.dot(attended, score_weight, precision=hp)
        return attended.astype(jnp.bfloat16), head_score

    attn_out, head_score = lax.map(one_slot, jnp.arange(R, dtype=jnp.int32))
    divergence = sibling_kl(head_score, draft_logit[serve_order].astype(jnp.float32), parents[serve_order])
    return attn_out, divergence
```

```python
import functools
import math

import jax
import jax.numpy as jnp
from jax import lax
from jax.experimental import pallas as pl
from jax.experimental.pallas import tpu as pltpu
from jax.sharding import PartitionSpec as P

HD = 128


def ancestor_bits(mask_words):
    node_count = mask_words.shape[-2]
    node_ids = jnp.arange(node_count, dtype=jnp.int32)
    chosen = jnp.where(node_ids // 32 == 0, mask_words[..., 0:1], mask_words[..., 1:2])
    return jnp.right_shift(chosen, node_ids % 32) & 1 == 1


def sibling_kl(head_score, drafted, parent_ids):
    node_count = parent_ids.shape[1]
    groups = parent_ids + 1
    onehot = (groups[:, :, None] == jnp.arange(node_count, dtype=jnp.int32)).astype(jnp.float32)
    target = 4.0 * jnp.tanh(head_score / 4.0)
    hp = lax.Precision.HIGHEST
    target_sums = jnp.einsum("rnc,rn->rc", onehot, jnp.exp(target), precision=hp)
    draft_sums = jnp.einsum("rnc,rn->rc", onehot, jnp.exp(drafted), precision=hp)
    target_log = target - jnp.log(jnp.einsum("rnc,rc->rn", onehot, target_sums, precision=hp))
    draft_log = drafted - jnp.log(jnp.einsum("rnc,rc->rn", onehot, draft_sums, precision=hp))
    return jnp.sum(jnp.exp(target_log) * (target_log - draft_log), axis=1)


def tree_part(grouped, tree_keys, tree_values, visible, softmax_scale):
    scores = (
        jnp.einsum("rnkgd,rmkd->rkngm", grouped, tree_keys, preferred_element_type=jnp.float32)
        * softmax_scale
    )
    allowed = visible[:, None, :, None, :]
    row_top = jnp.max(jnp.where(allowed, scores, -jnp.inf), axis=-1)
    weights = jnp.where(allowed, jnp.exp(scores - row_top[..., None]), 0.0)
    totals = jnp.sum(weights, axis=-1)
    weighted = jnp.einsum(
        "rkngm,rmkd->rkngd",
        weights.astype(jnp.bfloat16),
        tree_values,
        preferred_element_type=jnp.float32,
    )
    return (row_top, totals, weighted)


def cache_part(carry_state, grouped, key_block, value_block, usable, softmax_scale):
    row_top, totals, weighted = carry_state
    scores = (
        jnp.einsum("rnkgd,rckd->rkngc", grouped, key_block, preferred_element_type=jnp.float32)
        * softmax_scale
    )
    allowed = usable[:, None, None, None, :]
    block_top = jnp.max(jnp.where(allowed, scores, -jnp.inf), axis=-1)
    new_top = jnp.maximum(row_top, block_top)
    factor = jnp.exp(row_top - new_top)
    weights = jnp.where(allowed, jnp.exp(scores - new_top[..., None]), 0.0)
    totals = totals * factor + jnp.sum(weights, axis=-1)
    weighted = weighted * factor[..., None] + jnp.einsum(
        "rkngc,rckd->rkngd",
        weights.astype(jnp.bfloat16),
        value_block,
        preferred_element_type=jnp.float32,
    )
    return (new_top, totals, weighted)


def block_walker(grouped, cache_keys, cache_values, cached_len, block_len, kv_local, softmax_scale):
    req_count = cache_keys.shape[0]

    def advance(block_id, carry_state):
        offset = block_id * block_len
        key_block = lax.dynamic_slice_in_dim(cache_keys, offset, block_len, 1).reshape(
            req_count, block_len, kv_local, HD
        )
        value_block = lax.dynamic_slice_in_dim(cache_values, offset, block_len, 1).reshape(
            req_count, block_len, kv_local, HD
        )
        usable = (offset + jnp.arange(block_len, dtype=jnp.int32))[None, :] < cached_len[:, None]
        return cache_part(carry_state, grouped, key_block, value_block, usable, softmax_scale)

    return advance


def attend(queries, tree_keys, tree_values, cache_keys, cache_values, cached_len, visible):
    req_count, node_count, feature_width = queries.shape
    kv_local = tree_keys.shape[2] // HD
    group_size = feature_width // (kv_local * HD)
    softmax_scale = HD ** (-0.5)
    grouped = queries.reshape(req_count, node_count, kv_local, group_size, HD)
    carry_state = tree_part(
        grouped,
        tree_keys.reshape(req_count, node_count, kv_local, HD),
        tree_values.reshape(req_count, node_count, kv_local, HD),
        visible,
        softmax_scale,
    )
    cache_len = cache_keys.shape[1]
    block_len = min(512, cache_len)
    block_count = cache_len // block_len
    advance = block_walker(
        grouped, cache_keys, cache_values, cached_len, block_len, kv_local, softmax_scale
    )
    carry_state = lax.fori_loop(0, block_count, advance, carry_state)
    row_top, totals, weighted = carry_state
    attended = weighted / totals[..., None]
    return jnp.transpose(attended, (0, 2, 1, 3, 4)).reshape(req_count, node_count, feature_width)


def pick_rows(rows, ids):
    chosen = [lax.dynamic_index_in_dim(rows, ids[i], 0, keepdims=True) for i in range(ids.shape[0])]
    return jnp.concatenate(chosen, axis=0)


def permute_requests(array, order):
    count = array.shape[0]
    onehot = (order[:, None] == jnp.arange(count, dtype=jnp.int32)).astype(array.dtype)
    moved = jnp.dot(onehot, array.reshape(count, -1), preferred_element_type=jnp.float32)
    return moved.astype(array.dtype).reshape(array.shape)


def body(
    tree_query,
    tree_key,
    tree_value,
    draft_logit,
    cache_key,
    cache_value,
    score_weight,
    serve_order,
    lengths,
    parents,
    ancestors,
):
    slots = cache_key.shape[0]
    first_slot = lax.axis_index("seq") * slots
    my_slots = lax.dynamic_slice_in_dim(serve_order, first_slot, slots)
    cached_len = pick_rows(lengths, my_slots)
    visible = ancestor_bits(pick_rows(ancestors, my_slots))
    own_parents = pick_rows(parents, my_slots)
    permuted_query = permute_requests(tree_query, serve_order)
    permuted_key = permute_requests(tree_key, serve_order)
    permuted_value = permute_requests(tree_value, serve_order)
    permuted_logit = permute_requests(draft_logit, serve_order)
    queries, tree_keys, tree_values, logits = (
        lax.all_to_all(permuted_query, "seq", split_axis=0, concat_axis=1, tiled=True),
        lax.all_to_all(permuted_key, "seq", split_axis=0, concat_axis=1, tiled=True),
        lax.all_to_all(permuted_value, "seq", split_axis=0, concat_axis=1, tiled=True),
        lax.all_to_all(permuted_logit, "seq", split_axis=0, concat_axis=1, tiled=True),
    )
    attended = attend(queries, tree_keys, tree_values, cache_key, cache_value, cached_len, visible)
    partial_score = jnp.sum(attended * score_weight[None, None, :], axis=2)
    head_score = lax.psum(partial_score, "tensor")
    divergence = sibling_kl(head_score, logits.astype(jnp.float32), own_parents)
    return (attended.astype(jnp.bfloat16), divergence)


MESH = pl.DeviceIdType.MESH


def attend_kernel(
    dims,
    order_ref,
    lengths_ref,
    query_hbm,
    key_hbm,
    value_hbm,
    logit_hbm,
    parent_hbm,
    anc_hbm,
    weight_hbm,
    cache_key_ref,
    cache_value_ref,
    out_ref,
    kl_ref,
    query_refs,
    key_ref,
    value_ref,
    logit_ref,
    parent_ref,
    anc_ref,
    weight_ref,
    send_q,
    recv_q,
    send_kv,
    recv_kv,
    kx,
    vx,
    bias,
    score_acc,
    send_logit,
    recv_logit,
    all_logit,
    same,
    draft_log,
    send_score,
    recv_score,
    q_send_sem,
    q_recv_sem,
    kv_send_sem,
    kv_recv_sem,
    cache_sem,
    logit_send_sem,
    logit_recv_sem,
    score_send_sem,
    score_recv_sem,
    load_sem,
    query_sem,
):
    count, shards, slots, part, cache_len, kv_local, group = dims
    nodes = count * part
    kv_width = kv_local * HD
    wide = group * HD
    units = slots * kv_local
    own = count - 1

    def load(source, target, place):
        return pltpu.make_async_copy(source, target, load_sem.at[place])

    loads = [
        load(key_hbm, key_ref, 0),
        load(value_hbm, value_ref, 1),
        load(logit_hbm, logit_ref, 2),
        load(anc_hbm, anc_ref, 3),
        load(parent_hbm, parent_ref, 4),
        load(weight_hbm, weight_ref, 5),
    ]
    query_loads = [
        pltpu.make_async_copy(
            query_hbm.at[:, :, pl.ds(k * wide, wide)],
            query_refs[k],
            query_sem.at[k],
        )
        for k in range(kv_local)
    ]
    loads[0].start()
    loads[1].start()
    loads[2].start()
    for copy in query_loads:
        copy.start()
    for copy in loads[3:]:
        copy.start()

    me = lax.axis_index("seq")
    shard = lax.axis_index("tensor")
    shard_peers = [(shard + 1 + p) % shards for p in range(shards - 1)]
    peers = [count - 1 - me, (me + count // 2) % count, me + 1 - 2 * (me % 2)]
    sources = peers + [me]

    barrier = pltpu.get_barrier_semaphore()
    for peer in peers:
        pl.semaphore_signal(barrier, inc=1, device_id={"seq": peer}, device_id_type=MESH)
    for peer in shard_peers:
        pl.semaphore_signal(barrier, inc=1, device_id={"tensor": peer}, device_id_type=MESH)

    def remote(source, target, send_sem, recv_sem, where):
        return pltpu.make_async_remote_copy(
            src_ref=source,
            dst_ref=target,
            send_sem=send_sem,
            recv_sem=recv_sem,
            device_id=where,
            device_id_type=MESH,
        )

    def kv_copy(place):
        return remote(
            send_kv.at[place],
            recv_kv.at[place],
            kv_send_sem.at[place],
            kv_recv_sem.at[place],
            {"seq": peers[place]},
        )

    def logit_copy(place):
        return remote(
            send_logit,
            recv_logit.at[place],
            logit_send_sem.at[place],
            logit_recv_sem.at[place],
            {"seq": peers[place]},
        )

    def score_copy(place):
        return remote(
            send_score,
            recv_score.at[shard],
            score_send_sem.at[place],
            score_recv_sem.at[shard],
            {"tensor": shard_peers[place]},
        )

    def q_copy(place, unit):
        return remote(
            send_q.at[place, unit],
            recv_q.at[place, unit],
            q_send_sem.at[place, unit],
            q_recv_sem.at[place, unit],
            {"seq": peers[place % own]},
        )

    def stage_kv(place, owner, target):
        for j in range(slots):
            request = order_ref[owner * slots + j]
            target[place, j, :, pl.ds(0, kv_width)] = key_ref[request]
            target[place, j, :, pl.ds(kv_width, kv_width)] = value_ref[request]

    def stage_q(place, unit, target):
        k, j = unit // slots, unit % slots
        request = order_ref[sources[place] * slots + j]
        target[place, unit] = query_refs[k][request]

    loads[0].wait()
    loads[1].wait()
    for place in range(own):
        stage_kv(place, peers[place], send_kv)
    pl.semaphore_wait(barrier, count + shards - 2)
    for place in range(own):
        kv_copy(place).start()

    sends = []
    for unit in range(units):
        sends += [(0, unit), (2, unit)]
    for unit in range(units):
        sends += [(1, unit)]
    loaded = 0
    cache_copies = []
    for k in range(kv_local):
        for j in range(slots):
            columns = pl.ds(k * HD, HD)
            cache_copies.append(
                pltpu.make_async_copy(
                    cache_key_ref.at[j, :, columns],
                    kx.at[j, k, pl.ds(0, cache_len), :],
                    cache_sem.at[0, j, k],
                )
            )
            cache_copies.append(
                pltpu.make_async_copy(
                    cache_value_ref.at[j, :, columns],
                    vx.at[j, k, pl.ds(0, cache_len), pl.ds(0, HD)],
                    cache_sem.at[1, j, k],
                )
            )
    for place, unit in sends:
        if unit // slots == loaded:
            query_loads[loaded].wait()
            loaded += 1
        stage_q(place, unit, send_q)
        q_copy(place, unit).start()
        if loaded == kv_local and cache_copies:
            for copy in cache_copies:
                copy.start()
            cache_copies = []
    loads[2].wait()
    into = lax.broadcasted_iota(jnp.int32, (part, HD), 1) == (
        lax.broadcasted_iota(jnp.int32, (part, HD), 0) + me * part
    )
    send_logit[...] = jnp.dot(
        logit_ref[...], into.astype(jnp.bfloat16), preferred_element_type=jnp.float32
    ).astype(jnp.bfloat16)
    for place in range(own):
        logit_copy(place).start()
    for unit in range(units):
        stage_q(own, unit, recv_q)
    stage_kv(own, me, recv_kv)

    for copy in loads[3:]:
        copy.wait()
    ones = jnp.ones((cache_len + HD, HD), jnp.bfloat16)
    key_id = lax.broadcasted_iota(jnp.int32, (HD, HD), 0)
    blank = jnp.zeros((1, HD - nodes), jnp.int32)
    square = (nodes, nodes)
    eye = lax.broadcasted_iota(jnp.int32, square, 0) == lax.broadcasted_iota(jnp.int32, square, 1)

    def upright(row):
        return jnp.sum(jnp.where(eye, row, 0.0), axis=1, keepdims=True)

    for j in range(slots):
        request = order_ref[me * slots + j]
        words = anc_ref[request]
        first = jnp.concatenate([words[0:1], blank], axis=1)
        second = jnp.concatenate([words[1:2], blank], axis=1)
        word = jnp.where(key_id < 32, first, second)
        seen = (lax.shift_right_logical(word, key_id % 32) & 1 == 1) & (key_id < nodes)
        bias[j] = jnp.transpose(jnp.where(seen, 0.0, -jnp.inf))[:nodes]
        for k in range(kv_local):
            vx[j, k, :, pl.ds(HD, HD)] = ones
            kx[j, k, pl.ds(cache_len + nodes, HD - nodes), :] = jnp.zeros((HD - nodes, HD), jnp.bfloat16)
            vx[j, k, pl.ds(cache_len + nodes, HD - nodes), pl.ds(0, HD)] = jnp.zeros(
                (HD - nodes, HD), jnp.bfloat16
            )
        parent = parent_ref[pl.ds(request, 1), :].astype(jnp.float32)
        same[j] = (upright(parent) == parent).astype(jnp.float32)
    send_score[...] = jnp.zeros_like(send_score)

    for place in range(own):
        kv_copy(place).wait_recv()
    for j in range(slots):
        for k in range(kv_local):
            for place in range(count):
                rows = pl.ds(pl.multiple_of(cache_len + sources[place] * part, part), part)
                kx[j, k, rows, :] = recv_kv[place, j, :, pl.ds(k * HD, HD)]
                vx[j, k, rows, pl.ds(0, HD)] = recv_kv[place, j, :, pl.ds(kv_width + k * HD, HD)]

    exponent = HD ** (-0.5) * math.log2(math.e)
    position = lax.broadcasted_iota(jnp.int32, (1, cache_len), 1)
    contract = (((1,), (1,)), ((), ()))

    def piece(place, unit, first_head, heads):
        k, j = unit // slots, unit % slots
        rows = pl.ds(pl.multiple_of(sources[place] * part, part), part)
        usable = position < lengths_ref[order_ref[me * slots + j]]
        tree_bias = jnp.concatenate([bias[j, rows, :]] * heads, axis=0)
        q = jnp.concatenate(
            [recv_q[place, unit, :, pl.ds((first_head + h) * HD, HD)] for h in range(heads)], axis=0
        )
        cache_scores = lax.dot_general(
            q, kx[j, k, pl.ds(0, cache_len), :], contract, preferred_element_type=jnp.float32
        )
        tree_scores = lax.dot_general(
            q, kx[j, k, pl.ds(cache_len, HD), :], contract, preferred_element_type=jnp.float32
        )
        cache_scores = jnp.where(usable, cache_scores, -jnp.inf)
        tree_scores = tree_scores + tree_bias
        top = jnp.maximum(
            jnp.max(cache_scores, axis=1, keepdims=True), jnp.max(tree_scores, axis=1, keepdims=True)
        ) * exponent
        cache_weights = jnp.exp2(cache_scores * exponent - top).astype(jnp.bfloat16)
        tree_weights = jnp.exp2(tree_scores * exponent - top).astype(jnp.bfloat16)
        weighted = jnp.dot(
            cache_weights, vx[j, k, pl.ds(0, cache_len), :], preferred_element_type=jnp.float32
        ) + jnp.dot(
            tree_weights, vx[j, k, pl.ds(cache_len, HD), :], preferred_element_type=jnp.float32
        )
        attended = weighted[:, :HD] / weighted[:, HD:]
        total = jnp.zeros((part, HD), jnp.float32)
        for h in range(heads):
            head = attended[h * part : (h + 1) * part]
            columns = pl.ds(pl.multiple_of((k * group + first_head + h) * HD, HD), HD)
            out_ref[j, rows, columns] = head.astype(jnp.bfloat16)
            total = total + head * weight_ref[k, :, pl.ds((first_head + h) * HD, HD)]
        return total

    def keep(place, unit, total):
        k, j = unit // slots, unit % slots
        rows = pl.ds(pl.multiple_of(sources[place] * part, part), part)
        score_acc[j, k, rows, :] = total

    def own_step(t, carry):
        for unit in (2 * t, 2 * t + 1):
            k, j = unit // slots, unit % slots
            pltpu.make_async_copy(
                cache_key_ref.at[0, :, pl.ds(0, HD)],
                kx.at[j, k, pl.ds(0, cache_len), :],
                cache_sem.at[0, j, k],
            ).wait()
            pltpu.make_async_copy(
                cache_value_ref.at[0, :, pl.ds(0, HD)],
                vx.at[j, k, pl.ds(0, cache_len), pl.ds(0, HD)],
                cache_sem.at[1, j, k],
            ).wait()
        totals = [piece(own, unit, 0, group) for unit in (2 * t, 2 * t + 1)]
        for unit, total in zip((2 * t, 2 * t + 1), totals):
            keep(own, unit, total)
        return carry

    def middle_step(unit, carry):
        q_copy(0, unit).wait_recv()
        q_copy(2, unit).wait_recv()
        totals = [piece(place, unit, 0, group) for place in (0, 2)]
        for place, total in zip((0, 2), totals):
            keep(place, unit, total)
        return carry

    def last_step(unit, carry):
        q_copy(1, unit).wait_recv()
        half = group // 2
        keep(1, unit, piece(1, unit, 0, half) + piece(1, unit, half, half))
        return carry

    lax.fori_loop(0, units // 2, own_step, 0)

    for place in range(own):
        logit_copy(place).wait_recv()
    logits = send_logit[...].astype(jnp.float32)
    for place in range(own):
        logits = logits + recv_logit[place].astype(jnp.float32)
    all_logit[...] = logits
    for j in range(slots):
        drafted = all_logit[pl.ds(order_ref[me * slots + j], 1), :][:, :nodes]
        sums = jnp.sum(same[j] * jnp.exp(drafted), axis=1, keepdims=True)
        draft_log[j] = upright(drafted) - jnp.log(sums)

    lax.fori_loop(0, units, middle_step, 0)
    lax.fori_loop(0, units, last_step, 0)
    partial_score = jnp.sum(jnp.sum(score_acc[...], axis=1), axis=-1)
    send_score[pl.ds(0, slots), pl.ds(0, nodes)] = partial_score
    for place in range(shards - 1):
        score_copy(place).start()
    head_score = partial_score
    for place in range(shards - 1):
        source = shard_peers[place]
        remote(
            send_score,
            recv_score.at[source],
            score_send_sem.at[place],
            score_recv_sem.at[source],
            {"tensor": source},
        ).wait_recv()
        head_score = head_score + recv_score[source, pl.ds(0, slots), pl.ds(0, nodes)]
    target = 4.0 * jnp.tanh(head_score / 4.0)
    for j in range(slots):
        row = target[j : j + 1]
        sums = jnp.sum(same[j] * jnp.exp(row), axis=1, keepdims=True)
        target_log = upright(row) - jnp.log(sums)
        kl_ref[j] = jnp.sum(jnp.exp(target_log) * (target_log - draft_log[j]))
    for place in range(shards - 1):
        score_copy(place).wait_send()
    for place in range(own):
        kv_copy(place).wait_send()
        logit_copy(place).wait_send()
        for unit in range(units):
            q_copy(place, unit).wait_send()


def fused_body(
    count,
    shards,
    tree_query,
    tree_key,
    tree_value,
    draft_logit,
    cache_key,
    cache_value,
    score_weight,
    serve_order,
    lengths,
    parents,
    ancestors,
):
    requests, part, width = tree_query.shape
    slots, cache_len, kv_width = cache_key.shape
    kv_local = kv_width // HD
    group = width // kv_width
    nodes = count * part
    dims = (count, shards, slots, part, cache_len, kv_local, group)
    vmem = pl.BlockSpec(memory_space=pltpu.VMEM)
    smem = pl.BlockSpec(memory_space=pltpu.SMEM)
    hbm = pl.BlockSpec(memory_space=pl.ANY)
    bf16, f32 = jnp.bfloat16, jnp.float32
    dma = pltpu.SemaphoreType.DMA
    places = max(shards - 1, 1)
    score_rows = -(-slots // 8) * 8
    wide = group * HD
    units = slots * kv_local
    return pl.pallas_call(
        functools.partial(attend_kernel, dims),
        name="tree_attend",
        out_shape=(
            pltpu.VMEM((slots, nodes, width), bf16),
            jax.ShapeDtypeStruct((slots,), f32),
        ),
        in_specs=[smem, smem, hbm, hbm, hbm, hbm, hbm, hbm, hbm, hbm, hbm],
        out_specs=(vmem, smem),
        scratch_shapes=[
            [pltpu.VMEM((requests, part, wide), bf16) for _ in range(kv_local)],
            pltpu.VMEM((requests, part, kv_width), bf16),
            pltpu.VMEM((requests, part, kv_width), bf16),
            pltpu.VMEM(draft_logit.shape, bf16),
            pltpu.VMEM(parents.shape, jnp.int32),
            pltpu.VMEM((requests, 2, nodes), jnp.int32),
            pltpu.VMEM((kv_local, 1, wide), f32),
            pltpu.VMEM((count - 1, units, part, wide), bf16),
            pltpu.VMEM((count, units, part, wide), bf16),
            pltpu.VMEM((count - 1, slots, part, 2 * kv_width), bf16),
            pltpu.VMEM((count, slots, part, 2 * kv_width), bf16),
            pltpu.VMEM((slots, kv_local, cache_len + HD, HD), bf16),
            pltpu.VMEM((slots, kv_local, cache_len + HD, 2 * HD), bf16),
            pltpu.VMEM((slots, nodes, HD), f32),
            pltpu.VMEM((slots, kv_local, nodes, HD), f32),
            pltpu.VMEM((requests, HD), bf16),
            pltpu.VMEM((count - 1, requests, HD), bf16),
            pltpu.VMEM((requests, HD), f32),
            pltpu.VMEM((slots, nodes, nodes), f32),
            pltpu.VMEM((slots, nodes, 1), f32),
            pltpu.VMEM((score_rows, HD), f32),
            pltpu.VMEM((shards, score_rows, HD), f32),
            dma((count - 1, units)),
            dma((count - 1, units)),
            dma((count - 1,)),
            dma((count - 1,)),
            dma((2, slots, kv_local)),
            dma((count - 1,)),
            dma((count - 1,)),
            dma((places,)),
            dma((shards,)),
            dma((6,)),
            dma((kv_local,)),
        ],
        compiler_params=pltpu.CompilerParams(
            collective_id=0, has_side_effects=True, vmem_limit_bytes=56 * 1024 * 1024
        ),
    )(
        serve_order,
        lengths,
        tree_query,
        tree_key,
        tree_value,
        draft_logit,
        parents,
        jnp.transpose(ancestors, (0, 2, 1)),
        score_weight.reshape(kv_local, 1, wide),
        cache_key,
        cache_value,
    )


def solution(mesh):
    count, shards = mesh.shape["seq"], mesh.shape["tensor"]

    def pick(tree_query, *others):
        nodes = tree_query.shape[1] * count
        slots = others[3].shape[0]
        if tree_query.shape[1] % 16 == 0 and count == 4 and nodes < HD and slots % 2 == 0:
            return fused_body(count, shards, tree_query, *others)
        return body(tree_query, *others)

    return jax.shard_map(
        pick,
        mesh=mesh,
        in_specs=(
            P("groups", "seq", "tensor"),
            P("groups", "seq", "tensor"),
            P("groups", "seq", "tensor"),
            P("groups", "seq"),
            P(("groups", "seq"), None, "tensor"),
            P(("groups", "seq"), None, "tensor"),
            P("tensor"),
            P("groups"),
            P("groups"),
            P("groups", None),
            P("groups", None, None),
        ),
        out_specs=(P(("groups", "seq"), None, "tensor"), P(("groups", "seq"))),
        check_vma=False,
    )
```

```python
import functools
import math

import jax
import jax.numpy as jnp
from jax import lax
from jax.experimental import pallas as pl
from jax.experimental.pallas import tpu as pltpu
from jax.sharding import PartitionSpec as P

HD = 128


def ancestor_bits(mask_words):
    node_count = mask_words.shape[-2]
    node_ids = jnp.arange(node_count, dtype=jnp.int32)
    chosen = jnp.where(node_ids // 32 == 0, mask_words[..., 0:1], mask_words[..., 1:2])
    return jnp.right_shift(chosen, node_ids % 32) & 1 == 1


def sibling_kl(head_score, drafted, parent_ids):
    node_count = parent_ids.shape[1]
    groups = parent_ids + 1
    onehot = (groups[:, :, None] == jnp.arange(node_count, dtype=jnp.int32)).astype(jnp.float32)
    target = 4.0 * jnp.tanh(head_score / 4.0)
    hp = lax.Precision.HIGHEST
    target_sums = jnp.einsum("rnc,rn->rc", onehot, jnp.exp(target), precision=hp)
    draft_sums = jnp.einsum("rnc,rn->rc", onehot, jnp.exp(drafted), precision=hp)
    target_log = target - jnp.log(jnp.einsum("rnc,rc->rn", onehot, target_sums, precision=hp))
    draft_log = drafted - jnp.log(jnp.einsum("rnc,rc->rn", onehot, draft_sums, precision=hp))
    return jnp.sum(jnp.exp(target_log) * (target_log - draft_log), axis=1)


def tree_part(grouped, tree_keys, tree_values, visible, softmax_scale):
    scores = (
        jnp.einsum("rnkgd,rmkd->rkngm", grouped, tree_keys, preferred_element_type=jnp.float32)
        * softmax_scale
    )
    allowed = visible[:, None, :, None, :]
    row_top = jnp.max(jnp.where(allowed, scores, -jnp.inf), axis=-1)
    weights = jnp.where(allowed, jnp.exp(scores - row_top[..., None]), 0.0)
    totals = jnp.sum(weights, axis=-1)
    weighted = jnp.einsum(
        "rkngm,rmkd->rkngd",
        weights.astype(jnp.bfloat16),
        tree_values,
        preferred_element_type=jnp.float32,
    )
    return (row_top, totals, weighted)


def cache_part(carry_state, grouped, key_block, value_block, usable, softmax_scale):
    row_top, totals, weighted = carry_state
    scores = (
        jnp.einsum("rnkgd,rckd->rkngc", grouped, key_block, preferred_element_type=jnp.float32)
        * softmax_scale
    )
    allowed = usable[:, None, None, None, :]
    block_top = jnp.max(jnp.where(allowed, scores, -jnp.inf), axis=-1)
    new_top = jnp.maximum(row_top, block_top)
    factor = jnp.exp(row_top - new_top)
    weights = jnp.where(allowed, jnp.exp(scores - new_top[..., None]), 0.0)
    totals = totals * factor + jnp.sum(weights, axis=-1)
    weighted = weighted * factor[..., None] + jnp.einsum(
        "rkngc,rckd->rkngd",
        weights.astype(jnp.bfloat16),
        value_block,
        preferred_element_type=jnp.float32,
    )
    return (new_top, totals, weighted)


def block_walker(grouped, cache_keys, cache_values, cached_len, block_len, kv_local, softmax_scale):
    req_count = cache_keys.shape[0]

    def advance(block_id, carry_state):
        offset = block_id * block_len
        key_block = lax.dynamic_slice_in_dim(cache_keys, offset, block_len, 1).reshape(
            req_count, block_len, kv_local, HD
        )
        value_block = lax.dynamic_slice_in_dim(cache_values, offset, block_len, 1).reshape(
            req_count, block_len, kv_local, HD
        )
        usable = (offset + jnp.arange(block_len, dtype=jnp.int32))[None, :] < cached_len[:, None]
        return cache_part(carry_state, grouped, key_block, value_block, usable, softmax_scale)

    return advance


def attend(queries, tree_keys, tree_values, cache_keys, cache_values, cached_len, visible):
    req_count, node_count, feature_width = queries.shape
    kv_local = tree_keys.shape[2] // HD
    group_size = feature_width // (kv_local * HD)
    softmax_scale = HD ** (-0.5)
    grouped = queries.reshape(req_count, node_count, kv_local, group_size, HD)
    carry_state = tree_part(
        grouped,
        tree_keys.reshape(req_count, node_count, kv_local, HD),
        tree_values.reshape(req_count, node_count, kv_local, HD),
        visible,
        softmax_scale,
    )
    cache_len = cache_keys.shape[1]
    block_len = min(512, cache_len)
    block_count = cache_len // block_len
    advance = block_walker(
        grouped, cache_keys, cache_values, cached_len, block_len, kv_local, softmax_scale
    )
    carry_state = lax.fori_loop(0, block_count, advance, carry_state)
    row_top, totals, weighted = carry_state
    attended = weighted / totals[..., None]
    return jnp.transpose(attended, (0, 2, 1, 3, 4)).reshape(req_count, node_count, feature_width)


def pick_rows(rows, ids):
    chosen = [lax.dynamic_index_in_dim(rows, ids[i], 0, keepdims=True) for i in range(ids.shape[0])]
    return jnp.concatenate(chosen, axis=0)


def permute_requests(array, order):
    count = array.shape[0]
    onehot = (order[:, None] == jnp.arange(count, dtype=jnp.int32)).astype(array.dtype)
    moved = jnp.dot(onehot, array.reshape(count, -1), preferred_element_type=jnp.float32)
    return moved.astype(array.dtype).reshape(array.shape)


def body(
    tree_query,
    tree_key,
    tree_value,
    draft_logit,
    cache_key,
    cache_value,
    score_weight,
    serve_order,
    lengths,
    parents,
    ancestors,
):
    slots = cache_key.shape[0]
    first_slot = lax.axis_index("seq") * slots
    my_slots = lax.dynamic_slice_in_dim(serve_order, first_slot, slots)
    cached_len = pick_rows(lengths, my_slots)
    visible = ancestor_bits(pick_rows(ancestors, my_slots))
    own_parents = pick_rows(parents, my_slots)
    permuted_query = permute_requests(tree_query, serve_order)
    permuted_key = permute_requests(tree_key, serve_order)
    permuted_value = permute_requests(tree_value, serve_order)
    permuted_logit = permute_requests(draft_logit, serve_order)
    queries, tree_keys, tree_values, logits = (
        lax.all_to_all(permuted_query, "seq", split_axis=0, concat_axis=1, tiled=True),
        lax.all_to_all(permuted_key, "seq", split_axis=0, concat_axis=1, tiled=True),
        lax.all_to_all(permuted_value, "seq", split_axis=0, concat_axis=1, tiled=True),
        lax.all_to_all(permuted_logit, "seq", split_axis=0, concat_axis=1, tiled=True),
    )
    attended = attend(queries, tree_keys, tree_values, cache_key, cache_value, cached_len, visible)
    partial_score = jnp.sum(attended * score_weight[None, None, :], axis=2)
    head_score = lax.psum(partial_score, "tensor")
    divergence = sibling_kl(head_score, logits.astype(jnp.float32), own_parents)
    return (attended.astype(jnp.bfloat16), divergence)


MESH = pl.DeviceIdType.MESH


def attend_kernel(
    dims,
    order_hbm,
    lengths_hbm,
    query_hbm,
    key_hbm,
    value_hbm,
    logit_hbm,
    parent_hbm,
    anc_hbm,
    weight_hbm,
    cache_key_ref,
    cache_value_ref,
    out_ref,
    kl_ref,
    order_ref,
    lengths_ref,
    query_refs,
    key_ref,
    value_ref,
    logit_ref,
    parent_ref,
    anc_ref,
    weight_ref,
    send_q,
    recv_q,
    send_kv,
    recv_kv,
    kx,
    vx,
    bias,
    score_acc,
    send_logit,
    recv_logit,
    all_logit,
    same,
    draft_log,
    send_score,
    recv_score,
    q_send_sem,
    q_recv_sem,
    kv_send_sem,
    kv_recv_sem,
    cache_sem,
    logit_send_sem,
    logit_recv_sem,
    score_send_sem,
    score_recv_sem,
    load_sem,
    query_sem,
):
    count, shards, slots, part, cache_len, kv_local, group = dims
    nodes = count * part
    kv_width = kv_local * HD
    wide = group * HD
    units = slots * kv_local
    own = count - 1

    def load(source, target, place):
        return pltpu.make_async_copy(source, target, load_sem.at[place])

    loads = [
        load(key_hbm, key_ref, 0),
        load(value_hbm, value_ref, 1),
        load(logit_hbm, logit_ref, 2),
        load(anc_hbm, anc_ref, 3),
        load(parent_hbm, parent_ref, 4),
        load(weight_hbm, weight_ref, 5),
        load(lengths_hbm, lengths_ref, 6),
        load(order_hbm, order_ref, 7),
    ]
    query_loads = [
        pltpu.make_async_copy(
            query_hbm.at[:, :, pl.ds(k * wide, wide)],
            query_refs[k],
            query_sem.at[k],
        )
        for k in range(kv_local)
    ]
    loads[7].start()
    loads[0].start()
    loads[1].start()
    loads[2].start()
    for copy in query_loads:
        copy.start()
    for copy in loads[3:7]:
        copy.start()

    me = lax.axis_index("seq")
    shard = lax.axis_index("tensor")
    shard_peers = [(shard + 1 + p) % shards for p in range(shards - 1)]
    lower = me < 2
    peers = [jnp.where(lower, 3, 0), jnp.where(lower, 2, 1), me + 1 - 2 * (me % 2)]
    across = jnp.where((me == 0) | (me == 3), 0, 1)
    slot_of = [across, across, 2]
    sources = peers + [me]

    barrier = pltpu.get_barrier_semaphore()
    for peer in peers:
        pl.semaphore_signal(barrier, inc=1, device_id={"seq": peer}, device_id_type=MESH)
    for peer in shard_peers:
        pl.semaphore_signal(barrier, inc=1, device_id={"tensor": peer}, device_id_type=MESH)

    def remote(source, target, send_sem, recv_sem, where):
        return pltpu.make_async_remote_copy(
            src_ref=source,
            dst_ref=target,
            send_sem=send_sem,
            recv_sem=recv_sem,
            device_id=where,
            device_id_type=MESH,
        )

    def kv_copy(place, slot):
        return remote(
            send_kv.at[place],
            recv_kv.at[slot],
            kv_send_sem.at[place],
            kv_recv_sem.at[slot],
            {"seq": peers[place]},
        )

    def logit_copy(place, slot):
        return remote(
            send_logit,
            recv_logit.at[slot],
            logit_send_sem.at[place],
            logit_recv_sem.at[slot],
            {"seq": peers[place]},
        )

    def score_copy(place):
        return remote(
            send_score,
            recv_score.at[shard],
            score_send_sem.at[place],
            score_recv_sem.at[shard],
            {"tensor": shard_peers[place]},
        )

    def q_copy(place, slot, unit):
        return remote(
            send_q.at[place, unit],
            recv_q.at[slot, unit],
            q_send_sem.at[place, unit],
            q_recv_sem.at[slot, unit],
            {"seq": peers[place]},
        )

    def stage_kv(place, owner, target):
        for j in range(slots):
            request = order_ref[owner * slots + j]
            target[place, j, :, pl.ds(0, kv_width)] = key_ref[request]
            target[place, j, :, pl.ds(kv_width, kv_width)] = value_ref[request]

    def stage_q(place, unit, target):
        k, j = unit // slots, unit % slots
        request = order_ref[sources[place] * slots + j]
        target[place, unit] = query_refs[k][request]

    loads[7].wait()
    loads[0].wait()
    loads[1].wait()
    for place in range(own):
        stage_kv(place, peers[place], send_kv)
    pl.semaphore_wait(barrier, count + shards - 2)
    for place in range(own):
        kv_copy(place, slot_of[place]).start()

    loads[2].wait()
    into = lax.broadcasted_iota(jnp.int32, (part, HD), 1) == (
        lax.broadcasted_iota(jnp.int32, (part, HD), 0) + me * part
    )
    send_logit[...] = jnp.dot(
        logit_ref[...], into.astype(jnp.bfloat16), preferred_element_type=jnp.float32
    ).astype(jnp.bfloat16)
    for place in range(own):
        logit_copy(place, slot_of[place]).start()
    sends = []
    for unit in range(units):
        sends += [(0, unit), (1, unit), (2, unit)]
    loaded = 0
    cache_copies = []
    for k in range(kv_local):
        for j in range(slots):
            columns = pl.ds(k * HD, HD)
            cache_copies.append(
                pltpu.make_async_copy(
                    cache_key_ref.at[j, :, columns],
                    kx.at[j, k, pl.ds(0, cache_len), :],
                    cache_sem.at[0, j, k],
                )
            )
            cache_copies.append(
                pltpu.make_async_copy(
                    cache_value_ref.at[j, :, columns],
                    vx.at[j, k, pl.ds(0, cache_len), pl.ds(0, HD)],
                    cache_sem.at[1, j, k],
                )
            )
    for place, unit in sends:
        if unit // slots == loaded:
            query_loads[loaded].wait()
            loaded += 1
        stage_q(place, unit, send_q)
        q_copy(place, slot_of[place], unit).start()
        if loaded == kv_local and cache_copies:
            for copy in cache_copies:
                copy.start()
            cache_copies = []
    for unit in range(units):
        stage_q(own, unit, recv_q)
    stage_kv(own, me, recv_kv)

    for copy in loads[3:7]:
        copy.wait()
    ones = jnp.ones((cache_len + HD, HD), jnp.bfloat16)
    key_id = lax.broadcasted_iota(jnp.int32, (HD, HD), 0)
    blank = jnp.zeros((1, HD - nodes), jnp.int32)
    square = (nodes, nodes)
    eye = lax.broadcasted_iota(jnp.int32, square, 0) == lax.broadcasted_iota(jnp.int32, square, 1)

    def upright(row):
        return jnp.sum(jnp.where(eye, row, 0.0), axis=1, keepdims=True)

    for j in range(slots):
        request = order_ref[me * slots + j]
        words = anc_ref[request]
        first = jnp.concatenate([words[0:1], blank], axis=1)
        second = jnp.concatenate([words[1:2], blank], axis=1)
        word = jnp.where(key_id < 32, first, second)
        seen = (lax.shift_right_logical(word, key_id % 32) & 1 == 1) & (key_id < nodes)
        bias[j] = jnp.transpose(jnp.where(seen, 0.0, -jnp.inf))[:nodes]
        for k in range(kv_local):
            vx[j, k, :, pl.ds(HD, HD)] = ones
            kx[j, k, pl.ds(cache_len + nodes, HD - nodes), :] = jnp.zeros((HD - nodes, HD), jnp.bfloat16)
            vx[j, k, pl.ds(cache_len + nodes, HD - nodes), pl.ds(0, HD)] = jnp.zeros(
                (HD - nodes, HD), jnp.bfloat16
            )
        parent = parent_ref[pl.ds(request, 1), :].astype(jnp.float32)
        same[j] = (upright(parent) == parent).astype(jnp.float32)
    send_score[...] = jnp.zeros_like(send_score)

    for place in range(own):
        kv_copy(place, place).wait_recv()
    for j in range(slots):
        for k in range(kv_local):
            for place in range(count):
                rows = pl.ds(pl.multiple_of(cache_len + sources[place] * part, part), part)
                kx[j, k, rows, :] = recv_kv[place, j, :, pl.ds(k * HD, HD)]
                vx[j, k, rows, pl.ds(0, HD)] = recv_kv[place, j, :, pl.ds(kv_width + k * HD, HD)]

    exponent = HD ** (-0.5) * math.log2(math.e)
    position = lax.broadcasted_iota(jnp.int32, (1, cache_len), 1)
    contract = (((1,), (1,)), ((), ()))

    def piece(place, unit, first_head, heads):
        k, j = unit // slots, unit % slots
        rows = pl.ds(pl.multiple_of(sources[place] * part, part), part)
        usable = position < lengths_ref[order_ref[me * slots + j]]
        tree_bias = jnp.concatenate([bias[j, rows, :]] * heads, axis=0)
        q = jnp.concatenate(
            [recv_q[place, unit, :, pl.ds((first_head + h) * HD, HD)] for h in range(heads)], axis=0
        )
        cache_scores = lax.dot_general(
            q, kx[j, k, pl.ds(0, cache_len), :], contract, preferred_element_type=jnp.float32
        )
        tree_scores = lax.dot_general(
            q, kx[j, k, pl.ds(cache_len, HD), :], contract, preferred_element_type=jnp.float32
        )
        cache_scores = jnp.where(usable, cache_scores, -jnp.inf)
        tree_scores = tree_scores + tree_bias
        top = jnp.maximum(
            jnp.max(cache_scores, axis=1, keepdims=True), jnp.max(tree_scores, axis=1, keepdims=True)
        ) * exponent
        cache_weights = jnp.exp2(cache_scores * exponent - top).astype(jnp.bfloat16)
        tree_weights = jnp.exp2(tree_scores * exponent - top).astype(jnp.bfloat16)
        weighted = jnp.dot(
            cache_weights, vx[j, k, pl.ds(0, cache_len), :], preferred_element_type=jnp.float32
        ) + jnp.dot(
            tree_weights, vx[j, k, pl.ds(cache_len, HD), :], preferred_element_type=jnp.float32
        )
        attended = weighted[:, :HD] / weighted[:, HD:]
        total = jnp.zeros((part, HD), jnp.float32)
        for h in range(heads):
            head = attended[h * part : (h + 1) * part]
            columns = pl.ds(pl.multiple_of((k * group + first_head + h) * HD, HD), HD)
            out_ref[j, rows, columns] = head.astype(jnp.bfloat16)
            total = total + head * weight_ref[k, :, pl.ds((first_head + h) * HD, HD)]
        return total

    def keep(place, unit, total):
        k, j = unit // slots, unit % slots
        rows = pl.ds(pl.multiple_of(sources[place] * part, part), part)
        score_acc[j, k, rows, :] = total

    def own_step(t, carry):
        for unit in (2 * t, 2 * t + 1):
            k, j = unit // slots, unit % slots
            pltpu.make_async_copy(
                cache_key_ref.at[0, :, pl.ds(0, HD)],
                kx.at[j, k, pl.ds(0, cache_len), :],
                cache_sem.at[0, j, k],
            ).wait()
            pltpu.make_async_copy(
                cache_value_ref.at[0, :, pl.ds(0, HD)],
                vx.at[j, k, pl.ds(0, cache_len), pl.ds(0, HD)],
                cache_sem.at[1, j, k],
            ).wait()
        totals = [piece(own, unit, 0, group) for unit in (2 * t, 2 * t + 1)]
        for unit, total in zip((2 * t, 2 * t + 1), totals):
            keep(own, unit, total)
        return carry

    half = group // 2

    def late_piece(unit):
        q_copy(1, 1, unit).wait_recv()
        keep(1, unit, piece(1, unit, 0, half) + piece(1, unit, half, half))

    def middle_step(unit, carry):
        q_copy(0, 0, unit).wait_recv()
        q_copy(2, 2, unit).wait_recv()
        totals = [piece(place, unit, 0, group) for place in (0, 2)]
        for place, total in zip((0, 2), totals):
            keep(place, unit, total)

        @pl.when((unit >= 3) & (unit % 2 == 1))
        def _():
            late_piece((unit - 2) // 2)

        return carry

    def last_step(unit, carry):
        late_piece(unit)
        return carry

    lax.fori_loop(0, units // 2, own_step, 0)

    lax.fori_loop(0, units, middle_step, 0)
    for place in range(own):
        logit_copy(place, place).wait_recv()
    logits = send_logit[...].astype(jnp.float32)
    for place in range(own):
        logits = logits + recv_logit[place].astype(jnp.float32)
    all_logit[...] = logits
    for j in range(slots):
        drafted = all_logit[pl.ds(order_ref[me * slots + j], 1), :][:, :nodes]
        sums = jnp.sum(same[j] * jnp.exp(drafted), axis=1, keepdims=True)
        draft_log[j] = upright(drafted) - jnp.log(sums)

    lax.fori_loop((units - 2) // 2, units, last_step, 0)
    partial_score = jnp.sum(jnp.sum(score_acc[...], axis=1), axis=-1)
    send_score[pl.ds(0, slots), pl.ds(0, nodes)] = partial_score
    for place in range(shards - 1):
        score_copy(place).start()
    head_score = partial_score
    for place in range(shards - 1):
        source = shard_peers[place]
        remote(
            send_score,
            recv_score.at[source],
            score_send_sem.at[place],
            score_recv_sem.at[source],
            {"tensor": source},
        ).wait_recv()
        head_score = head_score + recv_score[source, pl.ds(0, slots), pl.ds(0, nodes)]
    target = 4.0 * jnp.tanh(head_score / 4.0)
    lane = lax.broadcasted_iota(jnp.int32, (1, HD), 1)
    divergence = jnp.zeros((1, HD), jnp.float32)
    for j in range(slots):
        row = target[j : j + 1]
        sums = jnp.sum(same[j] * jnp.exp(row), axis=1, keepdims=True)
        target_log = upright(row) - jnp.log(sums)
        terms = jnp.exp(target_log) * (target_log - draft_log[j])
        divergence = jnp.where(lane == j, jnp.sum(terms, axis=0, keepdims=True), divergence)
    kl_ref[...] = divergence[:, :slots]
    for place in range(shards - 1):
        score_copy(place).wait_send()
    for place in range(own):
        kv_copy(place, place).wait_send()
        logit_copy(place, place).wait_send()
        for unit in range(units):
            q_copy(place, place, unit).wait_send()


def fused_body(
    count,
    shards,
    tree_query,
    tree_key,
    tree_value,
    draft_logit,
    cache_key,
    cache_value,
    score_weight,
    serve_order,
    lengths,
    parents,
    ancestors,
):
    requests, part, width = tree_query.shape
    slots, cache_len, kv_width = cache_key.shape
    kv_local = kv_width // HD
    group = width // kv_width
    nodes = count * part
    dims = (count, shards, slots, part, cache_len, kv_local, group)
    vmem = pl.BlockSpec(memory_space=pltpu.VMEM)
    hbm = pl.BlockSpec(memory_space=pl.ANY)
    bf16, f32 = jnp.bfloat16, jnp.float32
    dma = pltpu.SemaphoreType.DMA
    places = max(shards - 1, 1)
    score_rows = -(-slots // 8) * 8
    wide = group * HD
    units = slots * kv_local
    attn_out, divergence = pl.pallas_call(
        functools.partial(attend_kernel, dims),
        name="tree_attend",
        out_shape=(
            pltpu.VMEM((slots, nodes, width), bf16),
            pltpu.VMEM((1, slots), f32),
        ),
        in_specs=[hbm, hbm, hbm, hbm, hbm, hbm, hbm, hbm, hbm, hbm, hbm],
        out_specs=(vmem, vmem),
        scratch_shapes=[
            pltpu.SMEM((requests,), jnp.int32),
            pltpu.SMEM((requests,), jnp.int32),
            [pltpu.VMEM((requests, part, wide), bf16) for _ in range(kv_local)],
            pltpu.VMEM((requests, part, kv_width), bf16),
            pltpu.VMEM((requests, part, kv_width), bf16),
            pltpu.VMEM(draft_logit.shape, bf16),
            pltpu.VMEM(parents.shape, jnp.int32),
            pltpu.VMEM((requests, 2, nodes), jnp.int32),
            pltpu.VMEM((kv_local, 1, wide), f32),
            pltpu.VMEM((count - 1, units, part, wide), bf16),
            pltpu.VMEM((count, units, part, wide), bf16),
            pltpu.VMEM((count - 1, slots, part, 2 * kv_width), bf16),
            pltpu.VMEM((count, slots, part, 2 * kv_width), bf16),
            pltpu.VMEM((slots, kv_local, cache_len + HD, HD), bf16),
            pltpu.VMEM((slots, kv_local, cache_len + HD, 2 * HD), bf16),
            pltpu.VMEM((slots, nodes, HD), f32),
            pltpu.VMEM((slots, kv_local, nodes, HD), f32),
            pltpu.VMEM((requests, HD), bf16),
            pltpu.VMEM((count - 1, requests, HD), bf16),
            pltpu.VMEM((requests, HD), f32),
            pltpu.VMEM((slots, nodes, nodes), f32),
            pltpu.VMEM((slots, nodes, 1), f32),
            pltpu.VMEM((score_rows, HD), f32),
            pltpu.VMEM((shards, score_rows, HD), f32),
            dma((count - 1, units)),
            dma((count - 1, units)),
            dma((count - 1,)),
            dma((count - 1,)),
            dma((2, slots, kv_local)),
            dma((count - 1,)),
            dma((count - 1,)),
            dma((places,)),
            dma((shards,)),
            dma((8,)),
            dma((kv_local,)),
        ],
        compiler_params=pltpu.CompilerParams(
            collective_id=0, has_side_effects=True, vmem_limit_bytes=56 * 1024 * 1024
        ),
    )(
        serve_order,
        lengths,
        tree_query,
        tree_key,
        tree_value,
        draft_logit,
        parents,
        jnp.transpose(ancestors, (0, 2, 1)),
        score_weight.reshape(kv_local, 1, wide),
        cache_key,
        cache_value,
    )
    return attn_out, divergence.reshape(slots)


def solution(mesh):
    count, shards = mesh.shape["seq"], mesh.shape["tensor"]

    def pick(tree_query, *others):
        nodes = tree_query.shape[1] * count
        slots = others[3].shape[0]
        if tree_query.shape[1] % 16 == 0 and count == 4 and nodes < HD and slots % 2 == 0:
            return fused_body(count, shards, tree_query, *others)
        return body(tree_query, *others)

    return jax.shard_map(
        pick,
        mesh=mesh,
        in_specs=(
            P("groups", "seq", "tensor"),
            P("groups", "seq", "tensor"),
            P("groups", "seq", "tensor"),
            P("groups", "seq"),
            P(("groups", "seq"), None, "tensor"),
            P(("groups", "seq"), None, "tensor"),
            P("tensor"),
            P("groups"),
            P("groups"),
            P("groups", None),
            P("groups", None, None),
        ),
        out_specs=(P(("groups", "seq"), None, "tensor"), P(("groups", "seq"))),
        check_vma=False,
    )
```

```python
import functools
import math

import jax
import jax.numpy as jnp
from jax import lax
from jax.experimental import pallas as pl
from jax.experimental.pallas import tpu as pltpu
from jax.sharding import PartitionSpec as P

HD = 128


def ancestor_bits(mask_words):
    node_count = mask_words.shape[-2]
    node_ids = jnp.arange(node_count, dtype=jnp.int32)
    chosen = jnp.where(node_ids // 32 == 0, mask_words[..., 0:1], mask_words[..., 1:2])
    return jnp.right_shift(chosen, node_ids % 32) & 1 == 1


def sibling_kl(head_score, drafted, parent_ids):
    node_count = parent_ids.shape[1]
    groups = parent_ids + 1
    onehot = (groups[:, :, None] == jnp.arange(node_count, dtype=jnp.int32)).astype(jnp.float32)
    target = 4.0 * jnp.tanh(head_score / 4.0)
    hp = lax.Precision.HIGHEST
    target_sums = jnp.einsum("rnc,rn->rc", onehot, jnp.exp(target), precision=hp)
    draft_sums = jnp.einsum("rnc,rn->rc", onehot, jnp.exp(drafted), precision=hp)
    target_log = target - jnp.log(jnp.einsum("rnc,rc->rn", onehot, target_sums, precision=hp))
    draft_log = drafted - jnp.log(jnp.einsum("rnc,rc->rn", onehot, draft_sums, precision=hp))
    return jnp.sum(jnp.exp(target_log) * (target_log - draft_log), axis=1)


def tree_part(grouped, tree_keys, tree_values, visible, softmax_scale):
    scores = (
        jnp.einsum("rnkgd,rmkd->rkngm", grouped, tree_keys, preferred_element_type=jnp.float32)
        * softmax_scale
    )
    allowed = visible[:, None, :, None, :]
    row_top = jnp.max(jnp.where(allowed, scores, -jnp.inf), axis=-1)
    weights = jnp.where(allowed, jnp.exp(scores - row_top[..., None]), 0.0)
    totals = jnp.sum(weights, axis=-1)
    weighted = jnp.einsum(
        "rkngm,rmkd->rkngd",
        weights.astype(jnp.bfloat16),
        tree_values,
        preferred_element_type=jnp.float32,
    )
    return (row_top, totals, weighted)


def cache_part(carry_state, grouped, key_block, value_block, usable, softmax_scale):
    row_top, totals, weighted = carry_state
    scores = (
        jnp.einsum("rnkgd,rckd->rkngc", grouped, key_block, preferred_element_type=jnp.float32)
        * softmax_scale
    )
    allowed = usable[:, None, None, None, :]
    block_top = jnp.max(jnp.where(allowed, scores, -jnp.inf), axis=-1)
    new_top = jnp.maximum(row_top, block_top)
    factor = jnp.exp(row_top - new_top)
    weights = jnp.where(allowed, jnp.exp(scores - new_top[..., None]), 0.0)
    totals = totals * factor + jnp.sum(weights, axis=-1)
    weighted = weighted * factor[..., None] + jnp.einsum(
        "rkngc,rckd->rkngd",
        weights.astype(jnp.bfloat16),
        value_block,
        preferred_element_type=jnp.float32,
    )
    return (new_top, totals, weighted)


def block_walker(grouped, cache_keys, cache_values, cached_len, block_len, kv_local, softmax_scale):
    req_count = cache_keys.shape[0]

    def advance(block_id, carry_state):
        offset = block_id * block_len
        key_block = lax.dynamic_slice_in_dim(cache_keys, offset, block_len, 1).reshape(
            req_count, block_len, kv_local, HD
        )
        value_block = lax.dynamic_slice_in_dim(cache_values, offset, block_len, 1).reshape(
            req_count, block_len, kv_local, HD
        )
        usable = (offset + jnp.arange(block_len, dtype=jnp.int32))[None, :] < cached_len[:, None]
        return cache_part(carry_state, grouped, key_block, value_block, usable, softmax_scale)

    return advance


def attend(queries, tree_keys, tree_values, cache_keys, cache_values, cached_len, visible):
    req_count, node_count, feature_width = queries.shape
    kv_local = tree_keys.shape[2] // HD
    group_size = feature_width // (kv_local * HD)
    softmax_scale = HD ** (-0.5)
    grouped = queries.reshape(req_count, node_count, kv_local, group_size, HD)
    carry_state = tree_part(
        grouped,
        tree_keys.reshape(req_count, node_count, kv_local, HD),
        tree_values.reshape(req_count, node_count, kv_local, HD),
        visible,
        softmax_scale,
    )
    cache_len = cache_keys.shape[1]
    block_len = min(512, cache_len)
    block_count = cache_len // block_len
    advance = block_walker(
        grouped, cache_keys, cache_values, cached_len, block_len, kv_local, softmax_scale
    )
    carry_state = lax.fori_loop(0, block_count, advance, carry_state)
    row_top, totals, weighted = carry_state
    attended = weighted / totals[..., None]
    return jnp.transpose(attended, (0, 2, 1, 3, 4)).reshape(req_count, node_count, feature_width)


def pick_rows(rows, ids):
    chosen = [lax.dynamic_index_in_dim(rows, ids[i], 0, keepdims=True) for i in range(ids.shape[0])]
    return jnp.concatenate(chosen, axis=0)


def permute_requests(array, order):
    count = array.shape[0]
    onehot = (order[:, None] == jnp.arange(count, dtype=jnp.int32)).astype(array.dtype)
    moved = jnp.dot(onehot, array.reshape(count, -1), preferred_element_type=jnp.float32)
    return moved.astype(array.dtype).reshape(array.shape)


def body(
    tree_query,
    tree_key,
    tree_value,
    draft_logit,
    cache_key,
    cache_value,
    score_weight,
    serve_order,
    lengths,
    parents,
    ancestors,
):
    slots = cache_key.shape[0]
    first_slot = lax.axis_index("seq") * slots
    my_slots = lax.dynamic_slice_in_dim(serve_order, first_slot, slots)
    cached_len = pick_rows(lengths, my_slots)
    visible = ancestor_bits(pick_rows(ancestors, my_slots))
    own_parents = pick_rows(parents, my_slots)
    permuted_query = permute_requests(tree_query, serve_order)
    permuted_key = permute_requests(tree_key, serve_order)
    permuted_value = permute_requests(tree_value, serve_order)
    permuted_logit = permute_requests(draft_logit, serve_order)
    queries, tree_keys, tree_values, logits = (
        lax.all_to_all(permuted_query, "seq", split_axis=0, concat_axis=1, tiled=True),
        lax.all_to_all(permuted_key, "seq", split_axis=0, concat_axis=1, tiled=True),
        lax.all_to_all(permuted_value, "seq", split_axis=0, concat_axis=1, tiled=True),
        lax.all_to_all(permuted_logit, "seq", split_axis=0, concat_axis=1, tiled=True),
    )
    attended = attend(queries, tree_keys, tree_values, cache_key, cache_value, cached_len, visible)
    partial_score = jnp.sum(attended * score_weight[None, None, :], axis=2)
    head_score = lax.psum(partial_score, "tensor")
    divergence = sibling_kl(head_score, logits.astype(jnp.float32), own_parents)
    return (attended.astype(jnp.bfloat16), divergence)


MESH = pl.DeviceIdType.MESH


def upright(row):
    square = (row.shape[1], row.shape[1])
    eye = lax.broadcasted_iota(jnp.int32, square, 0) == lax.broadcasted_iota(jnp.int32, square, 1)
    return jnp.sum(jnp.where(eye, row, 0.0), axis=1, keepdims=True)


def finish_kernel(attended_ref, score_ref, same_ref, draft_ref, out_ref, kl_ref, kl_row, sem):
    slots = score_ref.shape[0]
    whole = pltpu.make_async_copy(attended_ref, out_ref, sem.at[0])
    whole.start()
    target = 4.0 * jnp.tanh(score_ref[...] / 4.0)
    lane = lax.broadcasted_iota(jnp.int32, (1, HD), 1)
    divergence = jnp.zeros((1, HD), jnp.float32)
    for j in range(slots):
        row = target[j : j + 1]
        sums = jnp.sum(same_ref[j] * jnp.exp(row), axis=1, keepdims=True)
        target_log = upright(row) - jnp.log(sums)
        terms = jnp.exp(target_log) * (target_log - draft_ref[j])
        divergence = jnp.where(lane == j, jnp.sum(terms, axis=0, keepdims=True), divergence)
    kl_row[...] = divergence[:, :slots]
    small = pltpu.make_async_copy(kl_row, kl_ref, sem.at[1])
    small.start()
    small.wait()
    whole.wait()


def attend_kernel(
    dims,
    order_hbm,
    lengths_hbm,
    query_hbm,
    key_hbm,
    value_hbm,
    logit_hbm,
    parent_hbm,
    anc_hbm,
    weight_hbm,
    cache_key_ref,
    cache_value_ref,
    out_ref,
    score_ref,
    same,
    draft_log,
    order_ref,
    lengths_ref,
    query_refs,
    key_ref,
    value_ref,
    logit_ref,
    parent_ref,
    anc_ref,
    weight_ref,
    send_q,
    recv_q,
    send_kv,
    recv_kv,
    kx,
    vx,
    bias,
    score_acc,
    send_logit,
    recv_logit,
    all_logit,
    send_score,
    recv_score,
    q_send_sem,
    q_recv_sem,
    kv_send_sem,
    kv_recv_sem,
    cache_sem,
    logit_send_sem,
    logit_recv_sem,
    score_send_sem,
    score_recv_sem,
    load_sem,
    query_sem,
):
    count, shards, slots, part, cache_len, kv_local, group = dims
    nodes = count * part
    kv_width = kv_local * HD
    wide = group * HD
    units = slots * kv_local
    own = count - 1

    me = lax.axis_index("seq")
    shard = lax.axis_index("tensor")
    shard_peers = [(shard + 1 + p) % shards for p in range(shards - 1)]
    lower = me < 2
    sources = [jnp.where(lower, 3, 0), jnp.where(lower, 2, 1), me + 1 - 2 * (me % 2), me]
    peers = [p + jnp.where(me <= p, 1, 0) for p in range(own)]
    across = jnp.where((me == 0) | (me == 3), 0, 1)
    slot_of = [jnp.where((peer < 2) == lower, 2, across) for peer in peers]

    barrier = pltpu.get_barrier_semaphore()
    for peer in peers:
        pl.semaphore_signal(barrier, inc=1, device_id={"seq": peer}, device_id_type=MESH)
    for peer in shard_peers:
        pl.semaphore_signal(barrier, inc=1, device_id={"tensor": peer}, device_id_type=MESH)

    def load(source, target, place):
        return pltpu.make_async_copy(source, target, load_sem.at[place])

    loads = [
        load(key_hbm, key_ref, 0),
        load(value_hbm, value_ref, 1),
        load(logit_hbm, logit_ref, 2),
        load(anc_hbm, anc_ref, 3),
        load(parent_hbm, parent_ref, 4),
        load(weight_hbm, weight_ref, 5),
        load(lengths_hbm, lengths_ref, 6),
        load(order_hbm, order_ref, 7),
    ]
    query_loads = [
        pltpu.make_async_copy(
            query_hbm.at[:, :, pl.ds(k * wide, wide)],
            query_refs[k],
            query_sem.at[k],
        )
        for k in range(kv_local)
    ]
    loads[7].start()
    loads[0].start()
    loads[1].start()
    loads[2].start()
    for copy in query_loads:
        copy.start()
    for copy in loads[3:7]:
        copy.start()

    def remote(source, target, send_sem, recv_sem, where):
        return pltpu.make_async_remote_copy(
            src_ref=source,
            dst_ref=target,
            send_sem=send_sem,
            recv_sem=recv_sem,
            device_id=where,
            device_id_type=MESH,
        )

    def kv_copy(place, slot):
        return remote(
            send_kv.at[place],
            recv_kv.at[slot],
            kv_send_sem.at[place],
            kv_recv_sem.at[slot],
            {"seq": peers[place]},
        )

    def logit_copy(place, slot):
        return remote(
            send_logit,
            recv_logit.at[slot],
            logit_send_sem.at[place],
            logit_recv_sem.at[slot],
            {"seq": peers[place]},
        )

    def score_copy(place):
        return remote(
            send_score,
            recv_score.at[shard],
            score_send_sem.at[place],
            score_recv_sem.at[shard],
            {"tensor": shard_peers[place]},
        )

    def q_copy(place, slot, unit):
        return remote(
            send_q.at[place, unit],
            recv_q.at[slot, unit],
            q_send_sem.at[place, unit],
            q_recv_sem.at[slot, unit],
            {"seq": peers[place]},
        )

    def stage_kv(place, owner, target):
        for j in range(slots):
            request = order_ref[owner * slots + j]
            target[place, j, :, pl.ds(0, kv_width)] = key_ref[request]
            target[place, j, :, pl.ds(kv_width, kv_width)] = value_ref[request]

    def stage_q(place, owner, unit, target):
        k, j = unit // slots, unit % slots
        request = order_ref[owner * slots + j]
        target[place, unit] = query_refs[k][request]

    loads[7].wait()
    loads[0].wait()
    loads[1].wait()
    for place in range(own):
        stage_kv(place, peers[place], send_kv)
    pl.semaphore_wait(barrier, count + shards - 2)
    for place in range(own):
        kv_copy(place, slot_of[place]).start()

    sends = []
    lead = 1
    for t in range(units + lead):
        sends += [(p, t - lead * (p > 0)) for p in range(own) if 0 <= t - lead * (p > 0) < units]
    loaded = 0
    cache_copies = []
    for k in range(kv_local):
        for j in range(slots):
            columns = pl.ds(k * HD, HD)
            cache_copies.append(
                pltpu.make_async_copy(
                    cache_key_ref.at[j, :, columns],
                    kx.at[j, k, pl.ds(0, cache_len), :],
                    cache_sem.at[0, j, k],
                )
            )
            cache_copies.append(
                pltpu.make_async_copy(
                    cache_value_ref.at[j, :, columns],
                    vx.at[j, k, pl.ds(0, cache_len), pl.ds(0, HD)],
                    cache_sem.at[1, j, k],
                )
            )
    for place, unit in sends:
        if unit // slots == loaded:
            query_loads[loaded].wait()
            loaded += 1
        stage_q(place, peers[place], unit, send_q)
        q_copy(place, slot_of[place], unit).start()
        if loaded == kv_local and cache_copies:
            for copy in cache_copies:
                copy.start()
            cache_copies = []
    loads[2].wait()
    into = lax.broadcasted_iota(jnp.int32, (part, HD), 1) == (
        lax.broadcasted_iota(jnp.int32, (part, HD), 0) + me * part
    )
    send_logit[...] = jnp.dot(
        logit_ref[...], into.astype(jnp.bfloat16), preferred_element_type=jnp.float32
    ).astype(jnp.bfloat16)
    for place in range(own):
        logit_copy(place, slot_of[place]).start()
    for unit in range(units):
        stage_q(own, me, unit, recv_q)
    stage_kv(own, me, recv_kv)

    for copy in loads[3:7]:
        copy.wait()
    ones = jnp.ones((cache_len + HD, HD), jnp.bfloat16)
    key_id = lax.broadcasted_iota(jnp.int32, (HD, HD), 0)
    blank = jnp.zeros((1, HD - nodes), jnp.int32)
    for j in range(slots):
        request = order_ref[me * slots + j]
        words = anc_ref[request]
        first = jnp.concatenate([words[0:1], blank], axis=1)
        second = jnp.concatenate([words[1:2], blank], axis=1)
        word = jnp.where(key_id < 32, first, second)
        seen = (lax.shift_right_logical(word, key_id % 32) & 1 == 1) & (key_id < nodes)
        bias[j] = jnp.transpose(jnp.where(seen, 0.0, -jnp.inf))[:nodes]
        for k in range(kv_local):
            vx[j, k, :, pl.ds(HD, HD)] = ones
            kx[j, k, pl.ds(cache_len + nodes, HD - nodes), :] = jnp.zeros((HD - nodes, HD), jnp.bfloat16)
            vx[j, k, pl.ds(cache_len + nodes, HD - nodes), pl.ds(0, HD)] = jnp.zeros(
                (HD - nodes, HD), jnp.bfloat16
            )
        parent = parent_ref[pl.ds(request, 1), :].astype(jnp.float32)
        same[j] = (upright(parent) == parent).astype(jnp.float32)
    send_score[...] = jnp.zeros_like(send_score)

    for place in range(own):
        kv_copy(place, place).wait_recv()
    for j in range(slots):
        for k in range(kv_local):
            for place in range(count):
                rows = pl.ds(pl.multiple_of(cache_len + sources[place] * part, part), part)
                kx[j, k, rows, :] = recv_kv[place, j, :, pl.ds(k * HD, HD)]
                vx[j, k, rows, pl.ds(0, HD)] = recv_kv[place, j, :, pl.ds(kv_width + k * HD, HD)]

    exponent = HD ** (-0.5) * math.log2(math.e)
    position = lax.broadcasted_iota(jnp.int32, (1, cache_len), 1)
    contract = (((1,), (1,)), ((), ()))

    def piece(place, unit, first_head, heads):
        k, j = unit // slots, unit % slots
        rows = pl.ds(pl.multiple_of(sources[place] * part, part), part)
        usable = position < lengths_ref[order_ref[me * slots + j]]
        tree_bias = jnp.concatenate([bias[j, rows, :]] * heads, axis=0)
        q = jnp.concatenate(
            [recv_q[place, unit, :, pl.ds((first_head + h) * HD, HD)] for h in range(heads)], axis=0
        )
        cache_scores = lax.dot_general(
            q, kx[j, k, pl.ds(0, cache_len), :], contract, preferred_element_type=jnp.float32
        )
        tree_scores = lax.dot_general(
            q, kx[j, k, pl.ds(cache_len, HD), :], contract, preferred_element_type=jnp.float32
        )
        cache_scores = jnp.where(usable, cache_scores, -jnp.inf)
        tree_scores = tree_scores + tree_bias
        top = jnp.maximum(
            jnp.max(cache_scores, axis=1, keepdims=True), jnp.max(tree_scores, axis=1, keepdims=True)
        ) * exponent
        cache_weights = jnp.exp2(cache_scores * exponent - top).astype(jnp.bfloat16)
        tree_weights = jnp.exp2(tree_scores * exponent - top).astype(jnp.bfloat16)
        weighted = jnp.dot(
            cache_weights, vx[j, k, pl.ds(0, cache_len), :], preferred_element_type=jnp.float32
        ) + jnp.dot(
            tree_weights, vx[j, k, pl.ds(cache_len, HD), :], preferred_element_type=jnp.float32
        )
        attended = weighted[:, :HD] / weighted[:, HD:]
        total = jnp.zeros((part, HD), jnp.float32)
        for h in range(heads):
            head = attended[h * part : (h + 1) * part]
            columns = pl.ds(pl.multiple_of((k * group + first_head + h) * HD, HD), HD)
            out_ref[j, rows, columns] = head.astype(jnp.bfloat16)
            total = total + head * weight_ref[k, :, pl.ds((first_head + h) * HD, HD)]
        return total

    def keep(place, unit, total):
        k, j = unit // slots, unit % slots
        rows = pl.ds(pl.multiple_of(sources[place] * part, part), part)
        score_acc[j, k, rows, :] = total

    def own_step(t, carry):
        for unit in (2 * t, 2 * t + 1):
            k, j = unit // slots, unit % slots
            pltpu.make_async_copy(
                cache_key_ref.at[0, :, pl.ds(0, HD)],
                kx.at[j, k, pl.ds(0, cache_len), :],
                cache_sem.at[0, j, k],
            ).wait()
            pltpu.make_async_copy(
                cache_value_ref.at[0, :, pl.ds(0, HD)],
                vx.at[j, k, pl.ds(0, cache_len), pl.ds(0, HD)],
                cache_sem.at[1, j, k],
            ).wait()
        totals = [piece(own, unit, 0, group) for unit in (2 * t, 2 * t + 1)]
        for unit, total in zip((2 * t, 2 * t + 1), totals):
            keep(own, unit, total)
        return carry

    half = group // 2

    def late_piece(unit):
        q_copy(1, 1, unit).wait_recv()
        keep(1, unit, piece(1, unit, 0, half) + piece(1, unit, half, half))

    def middle_step(unit, carry):
        q_copy(0, 0, unit).wait_recv()
        q_copy(2, 2, unit).wait_recv()
        totals = [piece(place, unit, 0, group) for place in (0, 2)]
        for place, total in zip((0, 2), totals):
            keep(place, unit, total)

        @pl.when((unit >= 3) & (unit % 2 == 1))
        def _():
            late_piece((unit - 2) // 2)

        return carry

    def last_step(unit, carry):
        late_piece(unit)
        return carry

    lax.fori_loop(0, units // 2, own_step, 0)

    lax.fori_loop(0, units, middle_step, 0)
    lax.fori_loop((units - 2) // 2, units, last_step, 0)
    partial_score = jnp.sum(jnp.sum(score_acc[...], axis=1), axis=-1)
    send_score[pl.ds(0, slots), pl.ds(0, nodes)] = partial_score
    for place in range(shards - 1):
        score_copy(place).start()
    for place in range(own):
        logit_copy(place, place).wait_recv()
    logits = send_logit[...].astype(jnp.float32)
    for place in range(own):
        logits = logits + recv_logit[place].astype(jnp.float32)
    all_logit[...] = logits
    for j in range(slots):
        drafted = all_logit[pl.ds(order_ref[me * slots + j], 1), :][:, :nodes]
        sums = jnp.sum(same[j] * jnp.exp(drafted), axis=1, keepdims=True)
        draft_log[j] = upright(drafted) - jnp.log(sums)

    head_score = partial_score
    for place in range(shards - 1):
        source = shard_peers[place]
        remote(
            send_score,
            recv_score.at[source],
            score_send_sem.at[place],
            score_recv_sem.at[source],
            {"tensor": source},
        ).wait_recv()
        head_score = head_score + recv_score[source, pl.ds(0, slots), pl.ds(0, nodes)]
    score_ref[...] = head_score
    for place in range(shards - 1):
        score_copy(place).wait_send()
    for place in range(own):
        kv_copy(place, place).wait_send()
        logit_copy(place, place).wait_send()
        for unit in range(units):
            q_copy(place, place, unit).wait_send()


def fused_body(
    count,
    shards,
    tree_query,
    tree_key,
    tree_value,
    draft_logit,
    cache_key,
    cache_value,
    score_weight,
    serve_order,
    lengths,
    parents,
    ancestors,
):
    requests, part, width = tree_query.shape
    slots, cache_len, kv_width = cache_key.shape
    kv_local = kv_width // HD
    group = width // kv_width
    nodes = count * part
    dims = (count, shards, slots, part, cache_len, kv_local, group)
    vmem = pl.BlockSpec(memory_space=pltpu.VMEM)
    hbm = pl.BlockSpec(memory_space=pl.ANY)
    bf16, f32 = jnp.bfloat16, jnp.float32
    dma = pltpu.SemaphoreType.DMA
    places = max(shards - 1, 1)
    score_rows = -(-slots // 8) * 8
    wide = group * HD
    units = slots * kv_local
    attended, *scored = pl.pallas_call(
        functools.partial(attend_kernel, dims),
        name="tree_attend",
        out_shape=(
            pltpu.VMEM((slots, nodes, width), bf16),
            pltpu.VMEM((slots, nodes), f32),
            pltpu.VMEM((slots, nodes, nodes), f32),
            pltpu.VMEM((slots, nodes, 1), f32),
        ),
        in_specs=[hbm, hbm, hbm, hbm, hbm, hbm, hbm, hbm, hbm, hbm, hbm],
        out_specs=(vmem, vmem, vmem, vmem),
        scratch_shapes=[
            pltpu.SMEM((requests,), jnp.int32),
            pltpu.SMEM((requests,), jnp.int32),
            [pltpu.VMEM((requests, part, wide), bf16) for _ in range(kv_local)],
            pltpu.VMEM((requests, part, kv_width), bf16),
            pltpu.VMEM((requests, part, kv_width), bf16),
            pltpu.VMEM(draft_logit.shape, bf16),
            pltpu.VMEM(parents.shape, jnp.int32),
            pltpu.VMEM((requests, 2, nodes), jnp.int32),
            pltpu.VMEM((kv_local, 1, wide), f32),
            pltpu.VMEM((count - 1, units, part, wide), bf16),
            pltpu.VMEM((count, units, part, wide), bf16),
            pltpu.VMEM((count - 1, slots, part, 2 * kv_width), bf16),
            pltpu.VMEM((count, slots, part, 2 * kv_width), bf16),
            pltpu.VMEM((slots, kv_local, cache_len + HD, HD), bf16),
            pltpu.VMEM((slots, kv_local, cache_len + HD, 2 * HD), bf16),
            pltpu.VMEM((slots, nodes, HD), f32),
            pltpu.VMEM((slots, kv_local, nodes, HD), f32),
            pltpu.VMEM((requests, HD), bf16),
            pltpu.VMEM((count - 1, requests, HD), bf16),
            pltpu.VMEM((requests, HD), f32),
            pltpu.VMEM((score_rows, HD), f32),
            pltpu.VMEM((shards, score_rows, HD), f32),
            dma((count - 1, units)),
            dma((count - 1, units)),
            dma((count - 1,)),
            dma((count - 1,)),
            dma((2, slots, kv_local)),
            dma((count - 1,)),
            dma((count - 1,)),
            dma((places,)),
            dma((shards,)),
            dma((8,)),
            dma((kv_local,)),
        ],
        compiler_params=pltpu.CompilerParams(
            collective_id=0, has_side_effects=True, vmem_limit_bytes=56 * 1024 * 1024
        ),
    )(
        serve_order,
        lengths,
        tree_query,
        tree_key,
        tree_value,
        draft_logit,
        parents,
        jnp.transpose(ancestors, (0, 2, 1)),
        score_weight.reshape(kv_local, 1, wide),
        cache_key,
        cache_value,
    )
    attn_out, divergence = pl.pallas_call(
        finish_kernel,
        name="tree_finish",
        out_shape=(
            jax.ShapeDtypeStruct((slots, nodes, width), bf16),
            jax.ShapeDtypeStruct((1, slots), f32),
        ),
        in_specs=[hbm, vmem, vmem, vmem],
        out_specs=(hbm, hbm),
        scratch_shapes=[pltpu.VMEM((1, slots), f32), dma((2,))],
        compiler_params=pltpu.CompilerParams(vmem_limit_bytes=4 * 1024 * 1024),
    )(attended, *scored)
    return attn_out, divergence.reshape(slots)


def solution(mesh):
    count, shards = mesh.shape["seq"], mesh.shape["tensor"]

    def pick(tree_query, *others):
        nodes = tree_query.shape[1] * count
        slots = others[3].shape[0]
        if tree_query.shape[1] % 16 == 0 and count == 4 and nodes < HD and slots % 2 == 0:
            return fused_body(count, shards, tree_query, *others)
        return body(tree_query, *others)

    return jax.shard_map(
        pick,
        mesh=mesh,
        in_specs=(
            P("groups", "seq", "tensor"),
            P("groups", "seq", "tensor"),
            P("groups", "seq", "tensor"),
            P("groups", "seq"),
            P(("groups", "seq"), None, "tensor"),
            P(("groups", "seq"), None, "tensor"),
            P("tensor"),
            P("groups"),
            P("groups"),
            P("groups", None),
            P("groups", None, None),
        ),
        out_specs=(P(("groups", "seq"), None, "tensor"), P(("groups", "seq"))),
        check_vma=False,
    )
```

```python
import functools
import math

import jax
import jax.numpy as jnp
from jax import lax
from jax.experimental import pallas as pl
from jax.experimental.pallas import tpu as pltpu
from jax.sharding import PartitionSpec as P

HD = 128


def ancestor_bits(mask_words):
    node_count = mask_words.shape[-2]
    node_ids = jnp.arange(node_count, dtype=jnp.int32)
    chosen = jnp.where(node_ids // 32 == 0, mask_words[..., 0:1], mask_words[..., 1:2])
    return jnp.right_shift(chosen, node_ids % 32) & 1 == 1


def sibling_kl(head_score, drafted, parent_ids):
    node_count = parent_ids.shape[1]
    groups = parent_ids + 1
    onehot = (groups[:, :, None] == jnp.arange(node_count, dtype=jnp.int32)).astype(jnp.float32)
    target = 4.0 * jnp.tanh(head_score / 4.0)
    hp = lax.Precision.HIGHEST
    target_sums = jnp.einsum("rnc,rn->rc", onehot, jnp.exp(target), precision=hp)
    draft_sums = jnp.einsum("rnc,rn->rc", onehot, jnp.exp(drafted), precision=hp)
    target_log = target - jnp.log(jnp.einsum("rnc,rc->rn", onehot, target_sums, precision=hp))
    draft_log = drafted - jnp.log(jnp.einsum("rnc,rc->rn", onehot, draft_sums, precision=hp))
    return jnp.sum(jnp.exp(target_log) * (target_log - draft_log), axis=1)


def tree_part(grouped, tree_keys, tree_values, visible, softmax_scale):
    scores = (
        jnp.einsum("rnkgd,rmkd->rkngm", grouped, tree_keys, preferred_element_type=jnp.float32)
        * softmax_scale
    )
    allowed = visible[:, None, :, None, :]
    row_top = jnp.max(jnp.where(allowed, scores, -jnp.inf), axis=-1)
    weights = jnp.where(allowed, jnp.exp(scores - row_top[..., None]), 0.0)
    totals = jnp.sum(weights, axis=-1)
    weighted = jnp.einsum(
        "rkngm,rmkd->rkngd",
        weights.astype(jnp.bfloat16),
        tree_values,
        preferred_element_type=jnp.float32,
    )
    return (row_top, totals, weighted)


def cache_part(carry_state, grouped, key_block, value_block, usable, softmax_scale):
    row_top, totals, weighted = carry_state
    scores = (
        jnp.einsum("rnkgd,rckd->rkngc", grouped, key_block, preferred_element_type=jnp.float32)
        * softmax_scale
    )
    allowed = usable[:, None, None, None, :]
    block_top = jnp.max(jnp.where(allowed, scores, -jnp.inf), axis=-1)
    new_top = jnp.maximum(row_top, block_top)
    factor = jnp.exp(row_top - new_top)
    weights = jnp.where(allowed, jnp.exp(scores - new_top[..., None]), 0.0)
    totals = totals * factor + jnp.sum(weights, axis=-1)
    weighted = weighted * factor[..., None] + jnp.einsum(
        "rkngc,rckd->rkngd",
        weights.astype(jnp.bfloat16),
        value_block,
        preferred_element_type=jnp.float32,
    )
    return (new_top, totals, weighted)


def block_walker(grouped, cache_keys, cache_values, cached_len, block_len, kv_local, softmax_scale):
    req_count = cache_keys.shape[0]

    def advance(block_id, carry_state):
        offset = block_id * block_len
        key_block = lax.dynamic_slice_in_dim(cache_keys, offset, block_len, 1).reshape(
            req_count, block_len, kv_local, HD
        )
        value_block = lax.dynamic_slice_in_dim(cache_values, offset, block_len, 1).reshape(
            req_count, block_len, kv_local, HD
        )
        usable = (offset + jnp.arange(block_len, dtype=jnp.int32))[None, :] < cached_len[:, None]
        return cache_part(carry_state, grouped, key_block, value_block, usable, softmax_scale)

    return advance


def attend(queries, tree_keys, tree_values, cache_keys, cache_values, cached_len, visible):
    req_count, node_count, feature_width = queries.shape
    kv_local = tree_keys.shape[2] // HD
    group_size = feature_width // (kv_local * HD)
    softmax_scale = HD ** (-0.5)
    grouped = queries.reshape(req_count, node_count, kv_local, group_size, HD)
    carry_state = tree_part(
        grouped,
        tree_keys.reshape(req_count, node_count, kv_local, HD),
        tree_values.reshape(req_count, node_count, kv_local, HD),
        visible,
        softmax_scale,
    )
    cache_len = cache_keys.shape[1]
    block_len = min(512, cache_len)
    block_count = cache_len // block_len
    advance = block_walker(
        grouped, cache_keys, cache_values, cached_len, block_len, kv_local, softmax_scale
    )
    carry_state = lax.fori_loop(0, block_count, advance, carry_state)
    row_top, totals, weighted = carry_state
    attended = weighted / totals[..., None]
    return jnp.transpose(attended, (0, 2, 1, 3, 4)).reshape(req_count, node_count, feature_width)


def pick_rows(rows, ids):
    chosen = [lax.dynamic_index_in_dim(rows, ids[i], 0, keepdims=True) for i in range(ids.shape[0])]
    return jnp.concatenate(chosen, axis=0)


def permute_requests(array, order):
    count = array.shape[0]
    onehot = (order[:, None] == jnp.arange(count, dtype=jnp.int32)).astype(array.dtype)
    moved = jnp.dot(onehot, array.reshape(count, -1), preferred_element_type=jnp.float32)
    return moved.astype(array.dtype).reshape(array.shape)


def body(
    tree_query,
    tree_key,
    tree_value,
    draft_logit,
    cache_key,
    cache_value,
    score_weight,
    serve_order,
    lengths,
    parents,
    ancestors,
):
    slots = cache_key.shape[0]
    first_slot = lax.axis_index("seq") * slots
    my_slots = lax.dynamic_slice_in_dim(serve_order, first_slot, slots)
    cached_len = pick_rows(lengths, my_slots)
    visible = ancestor_bits(pick_rows(ancestors, my_slots))
    own_parents = pick_rows(parents, my_slots)
    permuted_query = permute_requests(tree_query, serve_order)
    permuted_key = permute_requests(tree_key, serve_order)
    permuted_value = permute_requests(tree_value, serve_order)
    permuted_logit = permute_requests(draft_logit, serve_order)
    queries, tree_keys, tree_values, logits = (
        lax.all_to_all(permuted_query, "seq", split_axis=0, concat_axis=1, tiled=True),
        lax.all_to_all(permuted_key, "seq", split_axis=0, concat_axis=1, tiled=True),
        lax.all_to_all(permuted_value, "seq", split_axis=0, concat_axis=1, tiled=True),
        lax.all_to_all(permuted_logit, "seq", split_axis=0, concat_axis=1, tiled=True),
    )
    attended = attend(queries, tree_keys, tree_values, cache_key, cache_value, cached_len, visible)
    partial_score = jnp.sum(attended * score_weight[None, None, :], axis=2)
    head_score = lax.psum(partial_score, "tensor")
    divergence = sibling_kl(head_score, logits.astype(jnp.float32), own_parents)
    return (attended.astype(jnp.bfloat16), divergence)


MESH = pl.DeviceIdType.MESH


def upright(row):
    square = (row.shape[1], row.shape[1])
    eye = lax.broadcasted_iota(jnp.int32, square, 0) == lax.broadcasted_iota(jnp.int32, square, 1)
    return jnp.sum(jnp.where(eye, row, 0.0), axis=1, keepdims=True)


def finish_kernel(attended_ref, score_ref, same_ref, draft_ref, out_ref, kl_ref, kl_row, sem):
    slots = score_ref.shape[0]
    whole = pltpu.make_async_copy(attended_ref, out_ref, sem.at[0])
    whole.start()
    target = 4.0 * jnp.tanh(score_ref[...] / 4.0)
    lane = lax.broadcasted_iota(jnp.int32, (1, HD), 1)
    divergence = jnp.zeros((1, HD), jnp.float32)
    for j in range(slots):
        row = target[j : j + 1]
        sums = jnp.sum(same_ref[j] * jnp.exp(row), axis=1, keepdims=True)
        target_log = upright(row) - jnp.log(sums)
        terms = jnp.exp(target_log) * (target_log - draft_ref[j])
        divergence = jnp.where(lane == j, jnp.sum(terms, axis=0, keepdims=True), divergence)
    kl_row[...] = divergence[:, :slots]
    small = pltpu.make_async_copy(kl_row, kl_ref, sem.at[1])
    small.start()
    small.wait()
    whole.wait()


def attend_kernel(
    dims,
    order_hbm,
    lengths_hbm,
    query_hbm,
    key_hbm,
    value_hbm,
    logit_hbm,
    parent_hbm,
    anc_hbm,
    weight_hbm,
    cache_key_ref,
    cache_value_ref,
    out_ref,
    score_ref,
    same,
    draft_log,
    order_ref,
    lengths_ref,
    query_refs,
    key_ref,
    value_ref,
    logit_ref,
    parent_ref,
    anc_ref,
    weight_ref,
    send_q,
    recv_q,
    send_kv,
    recv_kv,
    kx,
    vx,
    bias,
    score_acc,
    send_logit,
    recv_logit,
    all_logit,
    send_score,
    recv_score,
    q_send_sem,
    q_recv_sem,
    kv_send_sem,
    kv_recv_sem,
    cache_sem,
    logit_send_sem,
    logit_recv_sem,
    score_send_sem,
    score_recv_sem,
    load_sem,
    query_sem,
):
    count, shards, slots, part, cache_len, kv_local, group = dims
    nodes = count * part
    kv_width = kv_local * HD
    wide = group * HD
    units = slots * kv_local
    own = count - 1

    me = lax.axis_index("seq")
    shard = lax.axis_index("tensor")
    shard_peers = [(shard + 1 + p) % shards for p in range(shards - 1)]
    lower = me < 2
    sources = [jnp.where(lower, 3, 0), jnp.where(lower, 2, 1), me + 1 - 2 * (me % 2), me]
    peers = [p + jnp.where(me <= p, 1, 0) for p in range(own)]
    across = jnp.where((me == 0) | (me == 3), 0, 1)
    slot_of = [jnp.where((peer < 2) == lower, 2, across) for peer in peers]

    barrier = pltpu.get_barrier_semaphore()
    for peer in peers:
        pl.semaphore_signal(barrier, inc=1, device_id={"seq": peer}, device_id_type=MESH)
    for peer in shard_peers:
        pl.semaphore_signal(barrier, inc=1, device_id={"tensor": peer}, device_id_type=MESH)

    def load(source, target, place):
        return pltpu.make_async_copy(source, target, load_sem.at[place])

    loads = [
        load(key_hbm, key_ref, 0),
        load(value_hbm, value_ref, 1),
        load(logit_hbm, logit_ref, 2),
        load(anc_hbm, anc_ref, 3),
        load(parent_hbm, parent_ref, 4),
        load(weight_hbm, weight_ref, 5),
        load(lengths_hbm, lengths_ref, 6),
        load(order_hbm, order_ref, 7),
    ]
    query_loads = [
        pltpu.make_async_copy(
            query_hbm.at[:, :, pl.ds(k * wide, wide)],
            query_refs[k],
            query_sem.at[k],
        )
        for k in range(kv_local)
    ]
    loads[7].start()
    loads[0].start()
    loads[1].start()
    loads[2].start()
    for copy in query_loads:
        copy.start()
    for copy in loads[3:7]:
        copy.start()

    def remote(source, target, send_sem, recv_sem, where):
        return pltpu.make_async_remote_copy(
            src_ref=source,
            dst_ref=target,
            send_sem=send_sem,
            recv_sem=recv_sem,
            device_id=where,
            device_id_type=MESH,
        )

    def kv_copy(place, slot):
        return remote(
            send_kv.at[place],
            recv_kv.at[slot],
            kv_send_sem.at[place],
            kv_recv_sem.at[slot],
            {"seq": peers[place]},
        )

    def logit_copy(place, slot):
        return remote(
            send_logit,
            recv_logit.at[slot],
            logit_send_sem.at[place],
            logit_recv_sem.at[slot],
            {"seq": peers[place]},
        )

    def score_copy(place):
        return remote(
            send_score,
            recv_score.at[shard],
            score_send_sem.at[place],
            score_recv_sem.at[shard],
            {"tensor": shard_peers[place]},
        )

    def q_copy(place, slot, unit):
        return remote(
            send_q.at[place, unit],
            recv_q.at[slot, unit],
            q_send_sem.at[place, unit],
            q_recv_sem.at[slot, unit],
            {"seq": peers[place]},
        )

    def stage_kv(place, owner, target):
        for j in range(slots):
            request = order_ref[owner * slots + j]
            target[place, j, :, pl.ds(0, kv_width)] = key_ref[request]
            target[place, j, :, pl.ds(kv_width, kv_width)] = value_ref[request]

    def stage_q(place, owner, unit, target):
        k, j = unit // slots, unit % slots
        request = order_ref[owner * slots + j]
        target[place, unit] = query_refs[k][request]

    loads[7].wait()
    loads[0].wait()
    loads[1].wait()
    for place in range(own):
        stage_kv(place, peers[place], send_kv)
    pl.semaphore_wait(barrier, count + shards - 2)
    for place in range(own):
        kv_copy(place, slot_of[place]).start()

    sends = []
    for t in range(units + 1):
        sends += [(p, t - (p == 1)) for p in (0, 2, 1) if 0 <= t - (p == 1) < units]
    loaded = 0
    cache_copies = []
    for k in range(kv_local):
        for j in range(slots):
            columns = pl.ds(k * HD, HD)
            cache_copies.append(
                pltpu.make_async_copy(
                    cache_key_ref.at[j, :, columns],
                    kx.at[j, k, pl.ds(0, cache_len), :],
                    cache_sem.at[0, j, k],
                )
            )
            cache_copies.append(
                pltpu.make_async_copy(
                    cache_value_ref.at[j, :, columns],
                    vx.at[j, k, pl.ds(0, cache_len), pl.ds(0, HD)],
                    cache_sem.at[1, j, k],
                )
            )
    for place, unit in sends:
        if unit // slots == loaded:
            query_loads[loaded].wait()
            loaded += 1
        stage_q(place, peers[place], unit, send_q)
        q_copy(place, slot_of[place], unit).start()
        if loaded == kv_local and cache_copies:
            for copy in cache_copies:
                copy.start()
            cache_copies = []
    loads[2].wait()
    into = lax.broadcasted_iota(jnp.int32, (part, HD), 1) == (
        lax.broadcasted_iota(jnp.int32, (part, HD), 0) + me * part
    )
    send_logit[...] = jnp.dot(
        logit_ref[...], into.astype(jnp.bfloat16), preferred_element_type=jnp.float32
    ).astype(jnp.bfloat16)
    for place in range(own):
        logit_copy(place, slot_of[place]).start()
    for unit in range(units):
        stage_q(own, me, unit, recv_q)
    stage_kv(own, me, recv_kv)

    for copy in loads[3:7]:
        copy.wait()
    ones = jnp.ones((cache_len + HD, HD), jnp.bfloat16)
    key_id = lax.broadcasted_iota(jnp.int32, (HD, HD), 0)
    blank = jnp.zeros((1, HD - nodes), jnp.int32)
    for j in range(slots):
        request = order_ref[me * slots + j]
        words = anc_ref[request]
        first = jnp.concatenate([words[0:1], blank], axis=1)
        second = jnp.concatenate([words[1:2], blank], axis=1)
        word = jnp.where(key_id < 32, first, second)
        seen = (lax.shift_right_logical(word, key_id % 32) & 1 == 1) & (key_id < nodes)
        bias[j] = jnp.transpose(jnp.where(seen, 0.0, -jnp.inf))[:nodes]
        for k in range(kv_local):
            vx[j, k, :, pl.ds(HD, HD)] = ones
            kx[j, k, pl.ds(cache_len + nodes, HD - nodes), :] = jnp.zeros((HD - nodes, HD), jnp.bfloat16)
            vx[j, k, pl.ds(cache_len + nodes, HD - nodes), pl.ds(0, HD)] = jnp.zeros(
                (HD - nodes, HD), jnp.bfloat16
            )
        parent = parent_ref[pl.ds(request, 1), :].astype(jnp.float32)
        same[j] = (upright(parent) == parent).astype(jnp.float32)
    send_score[...] = jnp.zeros_like(send_score)

    for place in range(own):
        kv_copy(place, place).wait_recv()
    for j in range(slots):
        for k in range(kv_local):
            for place in range(count):
                rows = pl.ds(pl.multiple_of(cache_len + sources[place] * part, part), part)
                kx[j, k, rows, :] = recv_kv[place, j, :, pl.ds(k * HD, HD)]
                vx[j, k, rows, pl.ds(0, HD)] = recv_kv[place, j, :, pl.ds(kv_width + k * HD, HD)]

    exponent = HD ** (-0.5) * math.log2(math.e)
    position = lax.broadcasted_iota(jnp.int32, (1, cache_len), 1)
    contract = (((1,), (1,)), ((), ()))

    def piece(place, unit, first_head, heads):
        k, j = unit // slots, unit % slots
        rows = pl.ds(pl.multiple_of(sources[place] * part, part), part)
        usable = position < lengths_ref[order_ref[me * slots + j]]
        tree_bias = jnp.concatenate([bias[j, rows, :]] * heads, axis=0)
        q = jnp.concatenate(
            [recv_q[place, unit, :, pl.ds((first_head + h) * HD, HD)] for h in range(heads)], axis=0
        )
        cache_scores = lax.dot_general(
            q, kx[j, k, pl.ds(0, cache_len), :], contract, preferred_element_type=jnp.float32
        )
        tree_scores = lax.dot_general(
            q, kx[j, k, pl.ds(cache_len, HD), :], contract, preferred_element_type=jnp.float32
        )
        cache_scores = jnp.where(usable, cache_scores, -jnp.inf)
        tree_scores = tree_scores + tree_bias
        top = jnp.maximum(
            jnp.max(cache_scores, axis=1, keepdims=True), jnp.max(tree_scores, axis=1, keepdims=True)
        ) * exponent
        cache_weights = jnp.exp2(cache_scores * exponent - top).astype(jnp.bfloat16)
        tree_weights = jnp.exp2(tree_scores * exponent - top).astype(jnp.bfloat16)
        weighted = jnp.dot(
            cache_weights, vx[j, k, pl.ds(0, cache_len), :], preferred_element_type=jnp.float32
        ) + jnp.dot(
            tree_weights, vx[j, k, pl.ds(cache_len, HD), :], preferred_element_type=jnp.float32
        )
        attended = weighted[:, :HD] / weighted[:, HD:]
        total = jnp.zeros((part, HD), jnp.float32)
        for h in range(heads):
            head = attended[h * part : (h + 1) * part]
            columns = pl.ds(pl.multiple_of((k * group + first_head + h) * HD, HD), HD)
            out_ref[j, rows, columns] = head.astype(jnp.bfloat16)
            total = total + head * weight_ref[k, :, pl.ds((first_head + h) * HD, HD)]
        return total

    def keep(place, unit, total):
        k, j = unit // slots, unit % slots
        rows = pl.ds(pl.multiple_of(sources[place] * part, part), part)
        score_acc[j, k, rows, :] = total

    def own_step(t, carry):
        for unit in (2 * t, 2 * t + 1):
            k, j = unit // slots, unit % slots
            pltpu.make_async_copy(
                cache_key_ref.at[0, :, pl.ds(0, HD)],
                kx.at[j, k, pl.ds(0, cache_len), :],
                cache_sem.at[0, j, k],
            ).wait()
            pltpu.make_async_copy(
                cache_value_ref.at[0, :, pl.ds(0, HD)],
                vx.at[j, k, pl.ds(0, cache_len), pl.ds(0, HD)],
                cache_sem.at[1, j, k],
            ).wait()
        totals = [piece(own, unit, 0, group) for unit in (2 * t, 2 * t + 1)]
        for unit, total in zip((2 * t, 2 * t + 1), totals):
            keep(own, unit, total)
        return carry

    half = group // 2

    def late_piece(unit):
        q_copy(1, 1, unit).wait_recv()
        keep(1, unit, piece(1, unit, 0, half) + piece(1, unit, half, half))

    def middle_step(unit, carry):
        q_copy(0, 0, unit).wait_recv()
        q_copy(2, 2, unit).wait_recv()
        totals = [piece(place, unit, 0, group) for place in (0, 2)]
        for place, total in zip((0, 2), totals):
            keep(place, unit, total)

        @pl.when((unit >= 3) & (unit % 2 == 1))
        def _():
            late_piece((unit - 2) // 2)

        return carry

    def last_step(unit, carry):
        late_piece(unit)
        return carry

    lax.fori_loop(0, units // 2, own_step, 0)

    lax.fori_loop(0, units, middle_step, 0)
    lax.fori_loop((units - 2) // 2, units, last_step, 0)
    partial_score = jnp.sum(jnp.sum(score_acc[...], axis=1), axis=-1)
    send_score[pl.ds(0, slots), pl.ds(0, nodes)] = partial_score
    for place in range(shards - 1):
        score_copy(place).start()
    for place in range(own):
        logit_copy(place, place).wait_recv()
    logits = send_logit[...].astype(jnp.float32)
    for place in range(own):
        logits = logits + recv_logit[place].astype(jnp.float32)
    all_logit[...] = logits
    for j in range(slots):
        drafted = all_logit[pl.ds(order_ref[me * slots + j], 1), :][:, :nodes]
        sums = jnp.sum(same[j] * jnp.exp(drafted), axis=1, keepdims=True)
        draft_log[j] = upright(drafted) - jnp.log(sums)

    head_score = partial_score
    for place in range(shards - 1):
        source = shard_peers[place]
        remote(
            send_score,
            recv_score.at[source],
            score_send_sem.at[place],
            score_recv_sem.at[source],
            {"tensor": source},
        ).wait_recv()
        head_score = head_score + recv_score[source, pl.ds(0, slots), pl.ds(0, nodes)]
    score_ref[...] = head_score
    for place in range(shards - 1):
        score_copy(place).wait_send()
    for place in range(own):
        kv_copy(place, place).wait_send()
        logit_copy(place, place).wait_send()
        for unit in range(units):
            q_copy(place, place, unit).wait_send()


def fused_body(
    count,
    shards,
    tree_query,
    tree_key,
    tree_value,
    draft_logit,
    cache_key,
    cache_value,
    score_weight,
    serve_order,
    lengths,
    parents,
    ancestors,
):
    requests, part, width = tree_query.shape
    slots, cache_len, kv_width = cache_key.shape
    kv_local = kv_width // HD
    group = width // kv_width
    nodes = count * part
    dims = (count, shards, slots, part, cache_len, kv_local, group)
    vmem = pl.BlockSpec(memory_space=pltpu.VMEM)
    hbm = pl.BlockSpec(memory_space=pl.ANY)
    bf16, f32 = jnp.bfloat16, jnp.float32
    dma = pltpu.SemaphoreType.DMA
    places = max(shards - 1, 1)
    score_rows = -(-slots // 8) * 8
    wide = group * HD
    units = slots * kv_local
    attended, *scored = pl.pallas_call(
        functools.partial(attend_kernel, dims),
        name="tree_attend",
        out_shape=(
            pltpu.VMEM((slots, nodes, width), bf16),
            pltpu.VMEM((slots, nodes), f32),
            pltpu.VMEM((slots, nodes, nodes), f32),
            pltpu.VMEM((slots, nodes, 1), f32),
        ),
        in_specs=[hbm, hbm, hbm, hbm, hbm, hbm, hbm, hbm, hbm, hbm, hbm],
        out_specs=(vmem, vmem, vmem, vmem),
        scratch_shapes=[
            pltpu.SMEM((requests,), jnp.int32),
            pltpu.SMEM((requests,), jnp.int32),
            [pltpu.VMEM((requests, part, wide), bf16) for _ in range(kv_local)],
            pltpu.VMEM((requests, part, kv_width), bf16),
            pltpu.VMEM((requests, part, kv_width), bf16),
            pltpu.VMEM(draft_logit.shape, bf16),
            pltpu.VMEM(parents.shape, jnp.int32),
            pltpu.VMEM((requests, 2, nodes), jnp.int32),
            pltpu.VMEM((kv_local, 1, wide), f32),
            pltpu.VMEM((count - 1, units, part, wide), bf16),
            pltpu.VMEM((count, units, part, wide), bf16),
            pltpu.VMEM((count - 1, slots, part, 2 * kv_width), bf16),
            pltpu.VMEM((count, slots, part, 2 * kv_width), bf16),
            pltpu.VMEM((slots, kv_local, cache_len + HD, HD), bf16),
            pltpu.VMEM((slots, kv_local, cache_len + HD, 2 * HD), bf16),
            pltpu.VMEM((slots, nodes, HD), f32),
            pltpu.VMEM((slots, kv_local, nodes, HD), f32),
            pltpu.VMEM((requests, HD), bf16),
            pltpu.VMEM((count - 1, requests, HD), bf16),
            pltpu.VMEM((requests, HD), f32),
            pltpu.VMEM((score_rows, HD), f32),
            pltpu.VMEM((shards, score_rows, HD), f32),
            dma((count - 1, units)),
            dma((count - 1, units)),
            dma((count - 1,)),
            dma((count - 1,)),
            dma((2, slots, kv_local)),
            dma((count - 1,)),
            dma((count - 1,)),
            dma((places,)),
            dma((shards,)),
            dma((8,)),
            dma((kv_local,)),
        ],
        compiler_params=pltpu.CompilerParams(
            collective_id=0, has_side_effects=True, vmem_limit_bytes=56 * 1024 * 1024
        ),
    )(
        serve_order,
        lengths,
        tree_query,
        tree_key,
        tree_value,
        draft_logit,
        parents,
        jnp.transpose(ancestors, (0, 2, 1)),
        score_weight.reshape(kv_local, 1, wide),
        cache_key,
        cache_value,
    )
    attn_out, divergence = pl.pallas_call(
        finish_kernel,
        name="tree_finish",
        out_shape=(
            jax.ShapeDtypeStruct((slots, nodes, width), bf16),
            jax.ShapeDtypeStruct((1, slots), f32),
        ),
        in_specs=[hbm, vmem, vmem, vmem],
        out_specs=(hbm, hbm),
        scratch_shapes=[pltpu.VMEM((1, slots), f32), dma((2,))],
        compiler_params=pltpu.CompilerParams(vmem_limit_bytes=4 * 1024 * 1024),
    )(attended, *scored)
    return attn_out, divergence.reshape(slots)


def solution(mesh):
    count, shards = mesh.shape["seq"], mesh.shape["tensor"]

    def pick(tree_query, *others):
        nodes = tree_query.shape[1] * count
        slots = others[3].shape[0]
        if tree_query.shape[1] % 16 == 0 and count == 4 and nodes < HD and slots % 2 == 0:
            return fused_body(count, shards, tree_query, *others)
        return body(tree_query, *others)

    return jax.shard_map(
        pick,
        mesh=mesh,
        in_specs=(
            P("groups", "seq", "tensor"),
            P("groups", "seq", "tensor"),
            P("groups", "seq", "tensor"),
            P("groups", "seq"),
            P(("groups", "seq"), None, "tensor"),
            P(("groups", "seq"), None, "tensor"),
            P("tensor"),
            P("groups"),
            P("groups"),
            P("groups", None),
            P("groups", None, None),
        ),
        out_specs=(P(("groups", "seq"), None, "tensor"), P(("groups", "seq"))),
        check_vma=False,
    )
```

```python
import functools
import math

import jax
import jax.numpy as jnp
from jax import lax
from jax.experimental import pallas as pl
from jax.experimental.pallas import tpu as pltpu
from jax.sharding import PartitionSpec as P

HD = 128


def ancestor_bits(mask_words):
    node_count = mask_words.shape[-2]
    node_ids = jnp.arange(node_count, dtype=jnp.int32)
    chosen = jnp.where(node_ids // 32 == 0, mask_words[..., 0:1], mask_words[..., 1:2])
    return jnp.right_shift(chosen, node_ids % 32) & 1 == 1


def sibling_kl(head_score, drafted, parent_ids):
    node_count = parent_ids.shape[1]
    groups = parent_ids + 1
    onehot = (groups[:, :, None] == jnp.arange(node_count, dtype=jnp.int32)).astype(jnp.float32)
    target = 4.0 * jnp.tanh(head_score / 4.0)
    hp = lax.Precision.HIGHEST
    target_sums = jnp.einsum("rnc,rn->rc", onehot, jnp.exp(target), precision=hp)
    draft_sums = jnp.einsum("rnc,rn->rc", onehot, jnp.exp(drafted), precision=hp)
    target_log = target - jnp.log(jnp.einsum("rnc,rc->rn", onehot, target_sums, precision=hp))
    draft_log = drafted - jnp.log(jnp.einsum("rnc,rc->rn", onehot, draft_sums, precision=hp))
    return jnp.sum(jnp.exp(target_log) * (target_log - draft_log), axis=1)


def tree_part(grouped, tree_keys, tree_values, visible, softmax_scale):
    scores = (
        jnp.einsum("rnkgd,rmkd->rkngm", grouped, tree_keys, preferred_element_type=jnp.float32)
        * softmax_scale
    )
    allowed = visible[:, None, :, None, :]
    row_top = jnp.max(jnp.where(allowed, scores, -jnp.inf), axis=-1)
    weights = jnp.where(allowed, jnp.exp(scores - row_top[..., None]), 0.0)
    totals = jnp.sum(weights, axis=-1)
    weighted = jnp.einsum(
        "rkngm,rmkd->rkngd",
        weights.astype(jnp.bfloat16),
        tree_values,
        preferred_element_type=jnp.float32,
    )
    return (row_top, totals, weighted)


def cache_part(carry_state, grouped, key_block, value_block, usable, softmax_scale):
    row_top, totals, weighted = carry_state
    scores = (
        jnp.einsum("rnkgd,rckd->rkngc", grouped, key_block, preferred_element_type=jnp.float32)
        * softmax_scale
    )
    allowed = usable[:, None, None, None, :]
    block_top = jnp.max(jnp.where(allowed, scores, -jnp.inf), axis=-1)
    new_top = jnp.maximum(row_top, block_top)
    factor = jnp.exp(row_top - new_top)
    weights = jnp.where(allowed, jnp.exp(scores - new_top[..., None]), 0.0)
    totals = totals * factor + jnp.sum(weights, axis=-1)
    weighted = weighted * factor[..., None] + jnp.einsum(
        "rkngc,rckd->rkngd",
        weights.astype(jnp.bfloat16),
        value_block,
        preferred_element_type=jnp.float32,
    )
    return (new_top, totals, weighted)


def block_walker(grouped, cache_keys, cache_values, cached_len, block_len, kv_local, softmax_scale):
    req_count = cache_keys.shape[0]

    def advance(block_id, carry_state):
        offset = block_id * block_len
        key_block = lax.dynamic_slice_in_dim(cache_keys, offset, block_len, 1).reshape(
            req_count, block_len, kv_local, HD
        )
        value_block = lax.dynamic_slice_in_dim(cache_values, offset, block_len, 1).reshape(
            req_count, block_len, kv_local, HD
        )
        usable = (offset + jnp.arange(block_len, dtype=jnp.int32))[None, :] < cached_len[:, None]
        return cache_part(carry_state, grouped, key_block, value_block, usable, softmax_scale)

    return advance


def attend(queries, tree_keys, tree_values, cache_keys, cache_values, cached_len, visible):
    req_count, node_count, feature_width = queries.shape
    kv_local = tree_keys.shape[2] // HD
    group_size = feature_width // (kv_local * HD)
    softmax_scale = HD ** (-0.5)
    grouped = queries.reshape(req_count, node_count, kv_local, group_size, HD)
    carry_state = tree_part(
        grouped,
        tree_keys.reshape(req_count, node_count, kv_local, HD),
        tree_values.reshape(req_count, node_count, kv_local, HD),
        visible,
        softmax_scale,
    )
    cache_len = cache_keys.shape[1]
    block_len = min(512, cache_len)
    block_count = cache_len // block_len
    advance = block_walker(
        grouped, cache_keys, cache_values, cached_len, block_len, kv_local, softmax_scale
    )
    carry_state = lax.fori_loop(0, block_count, advance, carry_state)
    row_top, totals, weighted = carry_state
    attended = weighted / totals[..., None]
    return jnp.transpose(attended, (0, 2, 1, 3, 4)).reshape(req_count, node_count, feature_width)


def pick_rows(rows, ids):
    chosen = [lax.dynamic_index_in_dim(rows, ids[i], 0, keepdims=True) for i in range(ids.shape[0])]
    return jnp.concatenate(chosen, axis=0)


def permute_requests(array, order):
    count = array.shape[0]
    onehot = (order[:, None] == jnp.arange(count, dtype=jnp.int32)).astype(array.dtype)
    moved = jnp.dot(onehot, array.reshape(count, -1), preferred_element_type=jnp.float32)
    return moved.astype(array.dtype).reshape(array.shape)


def body(
    tree_query,
    tree_key,
    tree_value,
    draft_logit,
    cache_key,
    cache_value,
    score_weight,
    serve_order,
    lengths,
    parents,
    ancestors,
):
    slots = cache_key.shape[0]
    first_slot = lax.axis_index("seq") * slots
    my_slots = lax.dynamic_slice_in_dim(serve_order, first_slot, slots)
    cached_len = pick_rows(lengths, my_slots)
    visible = ancestor_bits(pick_rows(ancestors, my_slots))
    own_parents = pick_rows(parents, my_slots)
    permuted_query = permute_requests(tree_query, serve_order)
    permuted_key = permute_requests(tree_key, serve_order)
    permuted_value = permute_requests(tree_value, serve_order)
    permuted_logit = permute_requests(draft_logit, serve_order)
    queries, tree_keys, tree_values, logits = (
        lax.all_to_all(permuted_query, "seq", split_axis=0, concat_axis=1, tiled=True),
        lax.all_to_all(permuted_key, "seq", split_axis=0, concat_axis=1, tiled=True),
        lax.all_to_all(permuted_value, "seq", split_axis=0, concat_axis=1, tiled=True),
        lax.all_to_all(permuted_logit, "seq", split_axis=0, concat_axis=1, tiled=True),
    )
    attended = attend(queries, tree_keys, tree_values, cache_key, cache_value, cached_len, visible)
    partial_score = jnp.sum(attended * score_weight[None, None, :], axis=2)
    head_score = lax.psum(partial_score, "tensor")
    divergence = sibling_kl(head_score, logits.astype(jnp.float32), own_parents)
    return (attended.astype(jnp.bfloat16), divergence)


MESH = pl.DeviceIdType.MESH


def upright(row):
    square = (row.shape[1], row.shape[1])
    eye = lax.broadcasted_iota(jnp.int32, square, 0) == lax.broadcasted_iota(jnp.int32, square, 1)
    return jnp.sum(jnp.where(eye, row, 0.0), axis=1, keepdims=True)


def finish_kernel(attended_ref, score_ref, same_ref, draft_ref, out_ref, kl_ref, kl_row, sem):
    slots = score_ref.shape[0]
    whole = pltpu.make_async_copy(attended_ref, out_ref, sem.at[0])
    whole.start()
    target = 4.0 * jnp.tanh(score_ref[...] / 4.0)
    lane = lax.broadcasted_iota(jnp.int32, (1, HD), 1)
    divergence = jnp.zeros((1, HD), jnp.float32)
    for j in range(slots):
        row = target[j : j + 1]
        sums = jnp.sum(same_ref[j] * jnp.exp(row), axis=1, keepdims=True)
        target_log = upright(row) - jnp.log(sums)
        terms = jnp.exp(target_log) * (target_log - draft_ref[j])
        divergence = jnp.where(lane == j, jnp.sum(terms, axis=0, keepdims=True), divergence)
    kl_row[...] = divergence[:, :slots]
    small = pltpu.make_async_copy(kl_row, kl_ref, sem.at[1])
    small.start()
    small.wait()
    whole.wait()


def attend_kernel(
    dims,
    order_hbm,
    lengths_hbm,
    query_hbm,
    key_hbm,
    value_hbm,
    logit_hbm,
    parent_hbm,
    anc_hbm,
    weight_hbm,
    cache_key_ref,
    cache_value_ref,
    out_ref,
    score_ref,
    same,
    draft_log,
    order_ref,
    lengths_ref,
    query_refs,
    key_ref,
    value_ref,
    logit_ref,
    parent_ref,
    anc_ref,
    weight_ref,
    send_q,
    recv_q,
    send_kv,
    recv_kv,
    kx,
    vx,
    bias,
    score_acc,
    send_logit,
    recv_logit,
    all_logit,
    send_score,
    recv_score,
    q_send_sem,
    q_recv_sem,
    kv_send_sem,
    kv_recv_sem,
    cache_sem,
    logit_send_sem,
    logit_recv_sem,
    score_send_sem,
    score_recv_sem,
    load_sem,
    query_sem,
):
    count, shards, slots, part, cache_len, kv_local, group = dims
    nodes = count * part
    kv_width = kv_local * HD
    wide = group * HD
    units = slots * kv_local
    own = count - 1

    me = lax.axis_index("seq")
    shard = lax.axis_index("tensor")
    shard_peers = [(shard + 1 + p) % shards for p in range(shards - 1)]
    lower = me < 2
    sources = [jnp.where(lower, 3, 0), jnp.where(lower, 2, 1), me + 1 - 2 * (me % 2), me]
    peers = [jnp.where(lower, 2, 0), jnp.where(lower, 3, 1), sources[2]]
    across = jnp.where((me == 0) | (me == 3), 0, 1)
    slot_of = [jnp.where((peer < 2) == lower, 2, across) for peer in peers]

    barrier = pltpu.get_barrier_semaphore()
    for peer in peers:
        pl.semaphore_signal(barrier, inc=1, device_id={"seq": peer}, device_id_type=MESH)
    for peer in shard_peers:
        pl.semaphore_signal(barrier, inc=1, device_id={"tensor": peer}, device_id_type=MESH)

    def load(source, target, place):
        return pltpu.make_async_copy(source, target, load_sem.at[place])

    loads = [
        load(key_hbm, key_ref, 0),
        load(value_hbm, value_ref, 1),
        load(logit_hbm, logit_ref, 2),
        load(anc_hbm, anc_ref, 3),
        load(parent_hbm, parent_ref, 4),
        load(weight_hbm, weight_ref, 5),
        load(lengths_hbm, lengths_ref, 6),
        load(order_hbm, order_ref, 7),
    ]
    query_loads = [
        pltpu.make_async_copy(
            query_hbm.at[:, :, pl.ds(k * wide, wide)],
            query_refs[k],
            query_sem.at[k],
        )
        for k in range(kv_local)
    ]
    loads[7].start()
    loads[0].start()
    loads[1].start()
    loads[2].start()
    for copy in query_loads:
        copy.start()
    for copy in loads[3:7]:
        copy.start()

    def remote(source, target, send_sem, recv_sem, where):
        return pltpu.make_async_remote_copy(
            src_ref=source,
            dst_ref=target,
            send_sem=send_sem,
            recv_sem=recv_sem,
            device_id=where,
            device_id_type=MESH,
        )

    def kv_copy(place, slot):
        return remote(
            send_kv.at[place],
            recv_kv.at[slot],
            kv_send_sem.at[place],
            kv_recv_sem.at[slot],
            {"seq": peers[place]},
        )

    def logit_copy(place, slot):
        return remote(
            send_logit,
            recv_logit.at[slot],
            logit_send_sem.at[place],
            logit_recv_sem.at[slot],
            {"seq": peers[place]},
        )

    def score_copy(place):
        return remote(
            send_score,
            recv_score.at[shard],
            score_send_sem.at[place],
            score_recv_sem.at[shard],
            {"tensor": shard_peers[place]},
        )

    def q_copy(place, slot, unit):
        return remote(
            send_q.at[place, unit],
            recv_q.at[slot, unit],
            q_send_sem.at[place, unit],
            q_recv_sem.at[slot, unit],
            {"seq": peers[place]},
        )

    def stage_kv(place, owner, target):
        for j in range(slots):
            request = order_ref[owner * slots + j]
            target[place, j, :, pl.ds(0, kv_width)] = key_ref[request]
            target[place, j, :, pl.ds(kv_width, kv_width)] = value_ref[request]

    def stage_q(place, owner, unit, target):
        k, j = unit // slots, unit % slots
        request = order_ref[owner * slots + j]
        target[place, unit] = query_refs[k][request]

    loads[7].wait()
    loads[0].wait()
    loads[1].wait()
    for place in range(own):
        stage_kv(place, peers[place], send_kv)
    pl.semaphore_wait(barrier, count + shards - 2)
    for place in range(own):
        kv_copy(place, slot_of[place]).start()

    sends = []
    for t in range(units + 1):
        sends += [(p, t - (p == 1)) for p in (0, 2, 1) if 0 <= t - (p == 1) < units]
    loaded = 0
    cache_copies = []
    for k in range(kv_local):
        for j in range(slots):
            columns = pl.ds(k * HD, HD)
            cache_copies.append(
                pltpu.make_async_copy(
                    cache_key_ref.at[j, :, columns],
                    kx.at[j, k, pl.ds(0, cache_len), :],
                    cache_sem.at[0, j, k],
                )
            )
            cache_copies.append(
                pltpu.make_async_copy(
                    cache_value_ref.at[j, :, columns],
                    vx.at[j, k, pl.ds(0, cache_len), pl.ds(0, HD)],
                    cache_sem.at[1, j, k],
                )
            )
    for place, unit in sends:
        if unit // slots == loaded:
            query_loads[loaded].wait()
            loaded += 1
        stage_q(place, peers[place], unit, send_q)
        q_copy(place, slot_of[place], unit).start()
        if loaded == kv_local and cache_copies:
            for copy in cache_copies:
                copy.start()
            cache_copies = []
    loads[2].wait()
    into = lax.broadcasted_iota(jnp.int32, (part, HD), 1) == (
        lax.broadcasted_iota(jnp.int32, (part, HD), 0) + me * part
    )
    send_logit[...] = jnp.dot(
        logit_ref[...], into.astype(jnp.bfloat16), preferred_element_type=jnp.float32
    ).astype(jnp.bfloat16)
    for place in range(own):
        logit_copy(place, slot_of[place]).start()
    for unit in range(units):
        stage_q(own, me, unit, recv_q)
    stage_kv(own, me, recv_kv)

    for copy in loads[3:7]:
        copy.wait()
    ones = jnp.ones((cache_len + HD, HD), jnp.bfloat16)
    key_id = lax.broadcasted_iota(jnp.int32, (HD, HD), 0)
    blank = jnp.zeros((1, HD - nodes), jnp.int32)
    for j in range(slots):
        request = order_ref[me * slots + j]
        words = anc_ref[request]
        first = jnp.concatenate([words[0:1], blank], axis=1)
        second = jnp.concatenate([words[1:2], blank], axis=1)
        word = jnp.where(key_id < 32, first, second)
        seen = (lax.shift_right_logical(word, key_id % 32) & 1 == 1) & (key_id < nodes)
        bias[j] = jnp.transpose(jnp.where(seen, 0.0, -jnp.inf))[:nodes]
        for k in range(kv_local):
            vx[j, k, :, pl.ds(HD, HD)] = ones
            kx[j, k, pl.ds(cache_len + nodes, HD - nodes), :] = jnp.zeros((HD - nodes, HD), jnp.bfloat16)
            vx[j, k, pl.ds(cache_len + nodes, HD - nodes), pl.ds(0, HD)] = jnp.zeros(
                (HD - nodes, HD), jnp.bfloat16
            )
        parent = parent_ref[pl.ds(request, 1), :].astype(jnp.float32)
        same[j] = (upright(parent) == parent).astype(jnp.float32)
    send_score[...] = jnp.zeros_like(send_score)

    for place in range(own):
        kv_copy(place, place).wait_recv()
    for j in range(slots):
        for k in range(kv_local):
            for place in range(count):
                rows = pl.ds(pl.multiple_of(cache_len + sources[place] * part, part), part)
                kx[j, k, rows, :] = recv_kv[place, j, :, pl.ds(k * HD, HD)]
                vx[j, k, rows, pl.ds(0, HD)] = recv_kv[place, j, :, pl.ds(kv_width + k * HD, HD)]

    exponent = HD ** (-0.5) * math.log2(math.e)
    position = lax.broadcasted_iota(jnp.int32, (1, cache_len), 1)
    contract = (((1,), (1,)), ((), ()))

    def piece(place, unit, first_head, heads):
        k, j = unit // slots, unit % slots
        rows = pl.ds(pl.multiple_of(sources[place] * part, part), part)
        usable = position < lengths_ref[order_ref[me * slots + j]]
        tree_bias = jnp.concatenate([bias[j, rows, :]] * heads, axis=0)
        q = jnp.concatenate(
            [recv_q[place, unit, :, pl.ds((first_head + h) * HD, HD)] for h in range(heads)], axis=0
        )
        cache_scores = lax.dot_general(
            q, kx[j, k, pl.ds(0, cache_len), :], contract, preferred_element_type=jnp.float32
        )
        tree_scores = lax.dot_general(
            q, kx[j, k, pl.ds(cache_len, HD), :], contract, preferred_element_type=jnp.float32
        )
        attended = []
        size = heads * part // 1
        span = cache_len // 2
        for r in range(1):
            here = slice(r * size, (r + 1) * size)
            cached = jnp.where(usable, cache_scores[here], -jnp.inf)
            tree = tree_scores[here] + tree_bias[here]
            top = jnp.maximum(
                jnp.max(cached, axis=1, keepdims=True), jnp.max(tree, axis=1, keepdims=True)
            ) * exponent
            weights = jnp.exp2(tree * exponent - top).astype(jnp.bfloat16)
            weighted = jnp.dot(
                weights, vx[j, k, pl.ds(cache_len, HD), :], preferred_element_type=jnp.float32
            )
            for c in range(2):
                block = cached[:, c * span : (c + 1) * span]
                weights = jnp.exp2(block * exponent - top).astype(jnp.bfloat16)
                weighted = weighted + jnp.dot(
                    weights, vx[j, k, pl.ds(c * span, span), :], preferred_element_type=jnp.float32
                )
            attended.append(weighted[:, :HD] / weighted[:, HD:])
        attended = jnp.concatenate(attended, axis=0)
        total = jnp.zeros((part, HD), jnp.float32)
        for h in range(heads):
            head = attended[h * part : (h + 1) * part]
            columns = pl.ds(pl.multiple_of((k * group + first_head + h) * HD, HD), HD)
            out_ref[j, rows, columns] = head.astype(jnp.bfloat16)
            total = total + head * weight_ref[k, :, pl.ds((first_head + h) * HD, HD)]
        return total

    def keep(place, unit, total):
        k, j = unit // slots, unit % slots
        rows = pl.ds(pl.multiple_of(sources[place] * part, part), part)
        score_acc[j, k, rows, :] = total

    def own_step(t, carry):
        for unit in (2 * t, 2 * t + 1):
            k, j = unit // slots, unit % slots
            pltpu.make_async_copy(
                cache_key_ref.at[0, :, pl.ds(0, HD)],
                kx.at[j, k, pl.ds(0, cache_len), :],
                cache_sem.at[0, j, k],
            ).wait()
            pltpu.make_async_copy(
                cache_value_ref.at[0, :, pl.ds(0, HD)],
                vx.at[j, k, pl.ds(0, cache_len), pl.ds(0, HD)],
                cache_sem.at[1, j, k],
            ).wait()
        totals = [piece(own, unit, 0, group) for unit in (2 * t, 2 * t + 1)]
        for unit, total in zip((2 * t, 2 * t + 1), totals):
            keep(own, unit, total)
        return carry

    half = group // 2

    def late_piece(unit):
        q_copy(1, 1, unit).wait_recv()
        keep(1, unit, piece(1, unit, 0, half) + piece(1, unit, half, half))

    def middle_step(unit, carry):
        q_copy(0, 0, unit).wait_recv()
        q_copy(2, 2, unit).wait_recv()
        totals = [piece(place, unit, 0, group) for place in (0, 2)]
        for place, total in zip((0, 2), totals):
            keep(place, unit, total)

        @pl.when((unit >= 3) & (unit % 2 == 1))
        def _():
            late_piece((unit - 2) // 2)

        return carry

    def last_step(unit, carry):
        late_piece(unit)
        return carry

    lax.fori_loop(0, units // 2, own_step, 0)

    lax.fori_loop(0, units, middle_step, 0)
    lax.fori_loop((units - 2) // 2, units, last_step, 0)
    partial_score = jnp.sum(jnp.sum(score_acc[...], axis=1), axis=-1)
    send_score[pl.ds(0, slots), pl.ds(0, nodes)] = partial_score
    for place in range(shards - 1):
        score_copy(place).start()
    for place in range(own):
        logit_copy(place, place).wait_recv()
    logits = send_logit[...].astype(jnp.float32)
    for place in range(own):
        logits = logits + recv_logit[place].astype(jnp.float32)
    all_logit[...] = logits
    for j in range(slots):
        drafted = all_logit[pl.ds(order_ref[me * slots + j], 1), :][:, :nodes]
        sums = jnp.sum(same[j] * jnp.exp(drafted), axis=1, keepdims=True)
        draft_log[j] = upright(drafted) - jnp.log(sums)

    for place in range(own):
        kv_copy(place, place).wait_send()
        logit_copy(place, place).wait_send()
        for unit in range(units):
            q_copy(place, place, unit).wait_send()
    head_score = partial_score
    for place in range(shards - 1):
        source = shard_peers[place]
        remote(
            send_score,
            recv_score.at[source],
            score_send_sem.at[place],
            score_recv_sem.at[source],
            {"tensor": source},
        ).wait_recv()
        head_score = head_score + recv_score[source, pl.ds(0, slots), pl.ds(0, nodes)]
    score_ref[...] = head_score
    for place in range(shards - 1):
        score_copy(place).wait_send()


def fused_body(
    count,
    shards,
    tree_query,
    tree_key,
    tree_value,
    draft_logit,
    cache_key,
    cache_value,
    score_weight,
    serve_order,
    lengths,
    parents,
    ancestors,
):
    requests, part, width = tree_query.shape
    slots, cache_len, kv_width = cache_key.shape
    kv_local = kv_width // HD
    group = width // kv_width
    nodes = count * part
    dims = (count, shards, slots, part, cache_len, kv_local, group)
    vmem = pl.BlockSpec(memory_space=pltpu.VMEM)
    hbm = pl.BlockSpec(memory_space=pl.ANY)
    bf16, f32 = jnp.bfloat16, jnp.float32
    dma = pltpu.SemaphoreType.DMA
    places = max(shards - 1, 1)
    score_rows = -(-slots // 8) * 8
    wide = group * HD
    units = slots * kv_local
    attended, *scored = pl.pallas_call(
        functools.partial(attend_kernel, dims),
        name="tree_attend",
        out_shape=(
            pltpu.VMEM((slots, nodes, width), bf16),
            pltpu.VMEM((slots, nodes), f32),
            pltpu.VMEM((slots, nodes, nodes), f32),
            pltpu.VMEM((slots, nodes, 1), f32),
        ),
        in_specs=[hbm, hbm, hbm, hbm, hbm, hbm, hbm, hbm, hbm, hbm, hbm],
        out_specs=(vmem, vmem, vmem, vmem),
        scratch_shapes=[
            pltpu.SMEM((requests,), jnp.int32),
            pltpu.SMEM((requests,), jnp.int32),
            [pltpu.VMEM((requests, part, wide), bf16) for _ in range(kv_local)],
            pltpu.VMEM((requests, part, kv_width), bf16),
            pltpu.VMEM((requests, part, kv_width), bf16),
            pltpu.VMEM(draft_logit.shape, bf16),
            pltpu.VMEM(parents.shape, jnp.int32),
            pltpu.VMEM((requests, 2, nodes), jnp.int32),
            pltpu.VMEM((kv_local, 1, wide), f32),
            pltpu.VMEM((count - 1, units, part, wide), bf16),
            pltpu.VMEM((count, units, part, wide), bf16),
            pltpu.VMEM((count - 1, slots, part, 2 * kv_width), bf16),
            pltpu.VMEM((count, slots, part, 2 * kv_width), bf16),
            pltpu.VMEM((slots, kv_local, cache_len + HD, HD), bf16),
            pltpu.VMEM((slots, kv_local, cache_len + HD, 2 * HD), bf16),
            pltpu.VMEM((slots, nodes, HD), f32),
            pltpu.VMEM((slots, kv_local, nodes, HD), f32),
            pltpu.VMEM((requests, HD), bf16),
            pltpu.VMEM((count - 1, requests, HD), bf16),
            pltpu.VMEM((requests, HD), f32),
            pltpu.VMEM((score_rows, HD), f32),
            pltpu.VMEM((shards, score_rows, HD), f32),
            dma((count - 1, units)),
            dma((count - 1, units)),
            dma((count - 1,)),
            dma((count - 1,)),
            dma((2, slots, kv_local)),
            dma((count - 1,)),
            dma((count - 1,)),
            dma((places,)),
            dma((shards,)),
            dma((8,)),
            dma((kv_local,)),
        ],
        compiler_params=pltpu.CompilerParams(
            collective_id=0, has_side_effects=True, vmem_limit_bytes=56 * 1024 * 1024
        ),
    )(
        serve_order,
        lengths,
        tree_query,
        tree_key,
        tree_value,
        draft_logit,
        parents,
        jnp.transpose(ancestors, (0, 2, 1)),
        score_weight.reshape(kv_local, 1, wide),
        cache_key,
        cache_value,
    )
    attn_out, divergence = pl.pallas_call(
        finish_kernel,
        name="tree_finish",
        out_shape=(
            jax.ShapeDtypeStruct((slots, nodes, width), bf16),
            jax.ShapeDtypeStruct((1, slots), f32),
        ),
        in_specs=[hbm, vmem, vmem, vmem],
        out_specs=(hbm, hbm),
        scratch_shapes=[pltpu.VMEM((1, slots), f32), dma((2,))],
        compiler_params=pltpu.CompilerParams(vmem_limit_bytes=4 * 1024 * 1024),
    )(attended, *scored)
    return attn_out, divergence.reshape(slots)


def solution(mesh):
    count, shards = mesh.shape["seq"], mesh.shape["tensor"]

    def pick(tree_query, *others):
        nodes = tree_query.shape[1] * count
        slots = others[3].shape[0]
        if tree_query.shape[1] % 16 == 0 and count == 4 and nodes < HD and slots % 2 == 0:
            return fused_body(count, shards, tree_query, *others)
        return body(tree_query, *others)

    return jax.shard_map(
        pick,
        mesh=mesh,
        in_specs=(
            P("groups", "seq", "tensor"),
            P("groups", "seq", "tensor"),
            P("groups", "seq", "tensor"),
            P("groups", "seq"),
            P(("groups", "seq"), None, "tensor"),
            P(("groups", "seq"), None, "tensor"),
            P("tensor"),
            P("groups"),
            P("groups"),
            P("groups", None),
            P("groups", None, None),
        ),
        out_specs=(P(("groups", "seq"), None, "tensor"), P(("groups", "seq"))),
        check_vma=False,
    )
```
